512 devices in a mesh: wide: 64 (over y, z), blk: 8 (over x, core).
Axes of the slice: x: 4, y: 8, z: 8, core: 2. Of those that a mesh axis runs over, the one named last changes fastest.
Arguments:
- dual_rhs: float32 [64, 8, 64, 256], P('wide', 'blk'), may hold values from -6 to 6
- local_inverse: bfloat16 [64, 8, 512, 512], P('wide', 'blk'), as said below
- dirichlet: bfloat16 [64, 8, 512, 512], P('wide', 'blk'), as said below
- coarse_basis: bfloat16 [64, 8, 512, 256], P('wide', 'blk'), may hold values from -0.375 to 0.375
- coarse_inverse: float32 [64, 8, 64, 64], P('wide', 'blk'), as said below
- corner_slot: int32 [8, 64], P('blk'), may hold values from 0 to 63, each once within a row
- side_map: int32 [64, 8, 512], P('wide', 'blk'), may hold values from 0 to 511, each once within a row
- edge_flip: int32 [64, 8, 2], P('wide', 'blk'), may hold values 0 or 1
Outputs:
- multipliers: float32 [64, 8, 64, 256], P('wide', 'blk')
- residual: float32 [64, 8, 64, 256], P('wide', 'blk')
The draws below stay inside these ranges and needn't reach their ends.
Inputs may be any that keep to these rules, and one draw needn't show every extreme that they name: Each row of corner_slot lists every slot of the row once. Each patch's side_map names every local side unknown once. `local_inverse`: symmetric positive definite, each patch with its own row scales. `dirichlet`: symmetric positive definite, each patch with its own row scales. `coarse_inverse`: symmetric positive definite blocks.
All inputs are finite; a program needn't handle non-finite values. No bound on the sum of `edge_flip` on one device may be relied on, other than what follows from the above.
Results may differ from the reference program's by a relative error of at most 0.009.
Values may be sent and summed in bfloat16 or wider, within the bound.
A program may use at most 64 MiB of HBM per device.

```python
import jax
import jax.numpy as jnp
from jax import lax

EDGE = 128
CORNER = 64
LOADS = 64
ITERS = 2
N_WIDE = 64
N_BLK = 8


def symmetric_block(key, lead, order, low, high):
    key_scale, key_raw = jax.random.split(key)
    scale = jnp.exp(jax.random.uniform(key_scale, lead + (order,), jnp.float32, jnp.log(low), jnp.log(high)))
    raw = jax.random.uniform(key_raw, lead + (order, order), jnp.float32, -1.0, 1.0)
    couple = (raw + jnp.swapaxes(raw, -1, -2)) * (0.4 / order)
    identity = jnp.eye(order, dtype=jnp.float32)
    return scale[..., :, None] * scale[..., None, :] * (identity + couple)


def draw_local_inverse(key, part):
    low, high = (0.6, 1.6)
    return symmetric_block(jax.random.fold_in(key, 11), (N_WIDE, N_BLK), 4 * EDGE, low, high).astype(jnp.bfloat16)


def draw_dirichlet(key, part):
    low, high = (0.6, 1.6)
    return symmetric_block(jax.random.fold_in(key, 23), (N_WIDE, N_BLK), 4 * EDGE, low, high).astype(jnp.bfloat16)


def draw_coarse_inverse(key, part):
    low, high = (0.6, 1.6)
    return symmetric_block(jax.random.fold_in(key, 37), (N_WIDE, N_BLK), CORNER, low, high)


def set_ends(entries, rng, low, high):
    dims = entries.shape
    index_at = [jax.random.randint(jax.random.fold_in(rng, axis), (), 0, dims[axis]) for axis in range(len(dims))]
    entries = entries.at[tuple(index_at)].set(low)
    longest = dims.index(max(dims))
    index_at[longest] = (index_at[longest] + 1) % dims[longest]
    return entries.at[tuple(index_at)].set(high)


def block_scale(rng, shape, pieces, smallest, high):
    def one(axis_at, shards_of):
        draws = jax.random.uniform(jax.random.fold_in(jax.random.fold_in(rng, 6), axis_at), (shards_of,), jnp.float32, smallest / len(pieces), high / len(pieces))
        return jnp.repeat(jnp.exp(draws), shape[axis_at] // shards_of).reshape((-1,) + (1,) * (len(shape) - axis_at - 1))

    gain = one(*pieces[0])
    for cut in pieces[1:]:
        gain = gain * one(*cut)
    return gain


def normal_values(rng, dims, scale, most, cuts=(), kind=jnp.bfloat16):
    drawn = scale * jax.random.normal(rng, dims, jnp.float32)
    if cuts:
        drawn = drawn * block_scale(rng, dims, cuts, -0.22, 0.18)
    return jnp.clip(drawn, -most, most).astype(kind)


def setup_inputs(seed: int = 0) -> dict:
    key_list = jax.random.split(jax.random.key(seed), 9)
    dual_rhs = normal_values(key_list[0], (N_WIDE, N_BLK, LOADS, 2 * EDGE), 1.0, 6.0, ((0, 64), (1, 8)), jnp.float32)
    local_inverse = draw_local_inverse(jax.random.fold_in(key_list[8], 71), 0)
    dirichlet = draw_dirichlet(jax.random.fold_in(key_list[8], 71), 0)
    coarse_basis = normal_values(key_list[3], (N_WIDE, N_BLK, 4 * EDGE, 4 * CORNER), (4 * CORNER) ** -0.5, 0.375, ((0, 64), (1, 8)))
    coarse_inverse = draw_coarse_inverse(jax.random.fold_in(key_list[8], 71), 0)
    corner_slot = jax.vmap(lambda own: jax.random.permutation(own, N_WIDE))(jax.random.split(key_list[5], N_BLK)).reshape((N_BLK, N_WIDE)).astype(jnp.int32)
    side_map = jax.vmap(lambda own: jax.random.permutation(own, 4 * EDGE))(jax.random.split(key_list[6], N_WIDE * N_BLK)).reshape((N_WIDE, N_BLK, 4 * EDGE)).astype(jnp.int32)
    edge_flip = set_ends((jax.random.randint(key_list[7], (N_WIDE, N_BLK, 2), 0, 2) < 1).astype(jnp.int32), jax.random.fold_in(key_list[7], 1), 0, 1)
    return {"dual_rhs": dual_rhs, "local_inverse": local_inverse, "dirichlet": dirichlet, "coarse_basis": coarse_basis, "coarse_inverse": coarse_inverse, "corner_slot": corner_slot, "side_map": side_map, "edge_flip": edge_flip}


def flipped(x, flag):
    return jnp.where(flag[:, :, None, None] == 1, x[..., ::-1], x)


def reference(dual_rhs, local_inverse, dirichlet, coarse_basis, coarse_inverse, corner_slot, side_map, edge_flip):
    edge = EDGE
    corner = CORNER
    width = N_WIDE
    height = N_BLK
    column = jnp.arange(width)
    has_right = (column < width - 1).astype(jnp.float32)[:, None, None, None]
    flip_right = edge_flip[:, :, 0]
    flip_up = edge_flip[:, :, 1]
    shape_side = (width, height, LOADS, 4 * edge)
    order = jnp.broadcast_to(side_map[:, :, None, :].astype(jnp.int32), shape_side)
    inverse = jnp.broadcast_to(jnp.argsort(side_map, axis=-1).astype(jnp.int32)[:, :, None, :], shape_side)
    greens = local_inverse.astype(jnp.float32)
    stiff = dirichlet.astype(jnp.float32)
    basis = coarse_basis.astype(jnp.float32)
    slot_t = corner_slot.T.astype(jnp.int32)
    cinv_right = coarse_inverse[slot_t, jnp.arange(height)[None, :]]
    mask = jnp.concatenate([jnp.broadcast_to(has_right, (width, 1, 1, edge)), jnp.ones((width, 1, 1, edge), jnp.float32)], axis=3)

    def spread(lam):
        own_right = lam[..., :edge]
        own_up = lam[..., edge:]
        sent_right = flipped(own_right, flip_right)
        from_left = jnp.concatenate([jnp.zeros_like(sent_right[:1]), sent_right[:-1]], axis=0)
        from_below = jnp.roll(flipped(own_up, flip_up), 1, axis=1)
        canon = jnp.concatenate([-from_left, own_right, -from_below, own_up], axis=3)
        return jnp.take_along_axis(canon, inverse, axis=3).astype(jnp.bfloat16)

    def jumps(field):
        canon = jnp.take_along_axis(field, order, axis=3)
        left = canon[..., :edge]
        right = canon[..., edge:2 * edge]
        bottom = canon[..., 2 * edge:3 * edge]
        top = canon[..., 3 * edge:]
        from_right = jnp.concatenate([left[1:], jnp.zeros_like(left[:1])], axis=0)
        from_above = jnp.roll(bottom, -1, axis=1)
        jump_right = (right - flipped(from_right, flip_right)) * has_right
        jump_up = top - flipped(from_above, flip_up)
        return jnp.concatenate([jump_right, jump_up], axis=3)

    def coarse(spread_u):
        part = jnp.einsum("wblr,wbrc->wblc", spread_u.astype(jnp.float32), basis)
        low = part[..., :corner] + jnp.roll(part[..., 2 * corner:3 * corner], 1, axis=1)
        rgt = part[..., corner:2 * corner] + jnp.roll(part[..., 3 * corner:], 1, axis=1)
        low_next = jnp.concatenate([low[1:], jnp.zeros_like(low[:1])], axis=0)
        total = rgt + low_next
        z_right = jnp.einsum("wblc,wbcd->wbld", total, cinv_right, precision=lax.Precision.HIGHEST)
        z_left = jnp.concatenate([jnp.zeros_like(z_right[:1]), z_right[:-1]], axis=0)
        values = jnp.concatenate([z_left, z_right, jnp.roll(z_left, -1, axis=1), jnp.roll(z_right, -1, axis=1)], axis=3)
        values = values.astype(jnp.bfloat16)
        return jnp.einsum("wblc,wbrc->wblr", values.astype(jnp.float32), basis)

    def apply_dual(x):
        spread_u = spread(x)
        local = jnp.einsum("wblr,wbrs->wbls", spread_u.astype(jnp.float32), greens)
        return jumps(local + coarse(spread_u))

    def apply_precond(x):
        spread_u = spread(x)
        local = jnp.einsum("wblr,wbrs->wbls", spread_u.astype(jnp.float32), stiff)
        return 0.25 * jumps(local)

    def inner(a, b):
        return jnp.sum(a * b, axis=(0, 1, 3))

    residual = dual_rhs * mask
    precond = apply_precond(residual)
    direction = precond
    norm_now = inner(residual, precond)
    multipliers = jnp.zeros_like(residual)
    for step in range(ITERS):
        image = apply_dual(direction)
        alpha = norm_now / inner(direction, image)
        multipliers = multipliers + alpha[None, None, :, None] * direction
        residual = residual - alpha[None, None, :, None] * image
        if step + 1 < ITERS:
            precond = apply_precond(residual)
            norm_next = inner(residual, precond)
            direction = precond + (norm_next / norm_now)[None, None, :, None] * direction
            norm_now = norm_next
    return multipliers, residual
```

```python
import functools

import jax
import jax.numpy as jnp
from jax import lax
from jax.experimental import pallas as pl
from jax.experimental.pallas import tpu as pltpu
from jax.sharding import PartitionSpec as P

MESH = pl.DeviceIdType.MESH
F32 = jnp.float32
BF16 = jnp.bfloat16
LEFT, RIGHT, LOWER, UPPER = range(4)
LL, LR, UL, UR = range(4)


def halves(x):
    hi = x.astype(BF16)
    lo = (x - hi.astype(F32)).astype(BF16)
    return jnp.concatenate([hi, lo], axis=0)


def wide_dot(x, matrix, dims=(((1,), (0,)), ((), ()))):
    rows = x.shape[0]
    both = lax.dot_general(halves(x), matrix, dims, preferred_element_type=F32)
    return both[:rows] + both[rows:]


def packed(block):
    rows = block.shape[0] // 2
    return jnp.concatenate([block[:rows], block[rows:]], axis=1)


def unpacked(block):
    width = block.shape[1] // 2
    return jnp.concatenate([block[:, :width], block[:, width:]], axis=0)


def kernel(
    line,
    slot_ref,
    flip_ref,
    map_ref,
    rhs_ref,
    cinv_ref,
    stiff_hbm,
    greens_hbm,
    basis_hbm,
    mult_ref,
    res_ref,
    stiff_ref,
    greens_ref,
    basis_ref,
    load_sem,
    first_out,
    first_in,
    first_send,
    first_recv,
    side_out,
    side_in,
    side_send,
    side_recv,
    corner_out,
    horiz_in,
    vert_in,
    diag_in,
    corner_send,
    corner_recv,
    block_z,
    block_stage,
    block_y,
    block_own,
    block_up,
    block_send,
    block_recv,
    sum_out,
    sum_in,
    sum_send,
    sum_recv,
):
    loads = rhs_ref.shape[0]
    edge = rhs_ref.shape[1] // 2
    n_wide = lax.axis_size("wide")
    n_blk = lax.axis_size("blk")
    n_y = n_wide // line
    col = lax.axis_index("wide")
    row = lax.axis_index("blk")
    y, z = col // line, col % line
    right, left = (col + 1) % n_wide, (col + n_wide - 1) % n_wide
    above, below = (row + 1) % n_blk, (row + n_blk - 1) % n_blk

    loading = [
        pltpu.make_async_copy(source, target, load_sem.at[k])
        for k, (source, target) in enumerate(
            [(stiff_hbm, stiff_ref), (greens_hbm, greens_ref), (basis_hbm, basis_ref)]
        )
    ]
    for copy in loading:
        copy.start()

    along_z = [y * line + (z + d) % line for d in range(1, line)]
    along_y = [((y + d) % n_y) * line + z for d in range(1, n_y)]
    along_blk = [(row + d) % n_blk for d in range(1, n_blk)]

    barrier = pltpu.get_barrier_semaphore()
    friends = [(c, row) for c in along_z + along_y + [left, right]]
    friends += [(col, r) for r in along_blk]
    friends += [(c, r) for c in (left, right) for r in (below, above)]
    for friend in friends:
        pl.semaphore_signal(barrier, inc=1, device_id=friend, device_id_type=MESH)
    pl.semaphore_wait(barrier, len(friends))

    sends = []

    def send(source, target, send_sem, recv_sem, device):
        copy = pltpu.make_async_remote_copy(
            src_ref=source,
            dst_ref=target,
            send_sem=send_sem,
            recv_sem=recv_sem,
            device_id=device,
            device_id_type=MESH,
        )
        copy.start()
        sends.append(copy)
        return copy

    has_left = jnp.where(col > 0, 1.0, 0.0).astype(F32)
    has_right = jnp.where(col < n_wide - 1, 1.0, 0.0).astype(F32)

    own_right = rhs_ref[:, :edge] * has_right
    own_up = rhs_ref[:, edge:]
    first_out[0, :loads] = own_right
    first_out[1, :loads] = own_up
    for k in range(2):
        flag = flip_ref[0, k].astype(F32)
        first_out[k, loads:] = jnp.full((8, edge), 1.0, F32) * flag
    first = [
        send(first_out.at[k], first_in.at[k], first_send.at[k], first_recv.at[k], device)
        for k, device in enumerate([(right, row), (col, above)])
    ]

    block_own[0] = packed(cinv_ref[...]).astype(BF16)
    fetch_z = [
        send(block_own.at[0], block_z.at[z], block_send.at[0, d], block_recv.at[0, d], (c, row))
        for d, c in enumerate(along_z)
    ]
    block_z[z] = block_own[0]

    for copy in first:
        copy.wait_recv()

    index = jnp.broadcast_to(map_ref[...].astype(F32), (8, 4 * edge))
    rows_at = lax.broadcasted_iota(jnp.int32, (edge, edge), 0)
    lanes_at = lax.broadcasted_iota(jnp.int32, (edge, edge), 1)
    turn = jnp.where(rows_at + lanes_at == edge - 1, 1.0, 0.0).astype(F32)

    def oriented(part, flag):
        back = jnp.dot(part, turn, precision=lax.Precision.HIGHEST, preferred_element_type=F32)
        return jnp.where(flag > 0.5, back, part)

    index = jnp.concatenate(
        [
            oriented(index[:, :edge], first_in[0, loads:]),
            index[:, edge : 2 * edge],
            oriented(index[:, 2 * edge : 3 * edge], first_in[1, loads:]),
            index[:, 3 * edge :],
        ],
        axis=1,
    )
    total = 4 * edge
    lane = lax.broadcasted_iota(jnp.int32, (8, total), 1)
    sign = jnp.where((lane // edge) % 2 == 0, -1.0, 1.0).astype(F32)
    columns = jnp.transpose(jnp.concatenate([index, sign], axis=0))
    index_row = (index[:1] + 0.5).astype(jnp.int32)
    index_col = (columns[:, :1] + 0.5).astype(jnp.int32)
    perm_t = jnp.where(
        lax.broadcasted_iota(jnp.int32, (total, total), 0) == index_row, sign[:1], 0.0
    ).astype(BF16)
    perm = jnp.where(
        lax.broadcasted_iota(jnp.int32, (total, total), 1) == index_col, columns[:, 8:9], 0.0
    ).astype(BF16)

    def reordered(matrix):
        half = jnp.dot(perm, matrix, preferred_element_type=F32).astype(BF16)
        return jnp.dot(half, perm_t, preferred_element_type=F32)

    loading[0].wait()
    stiff_ref[...] = (0.25 * reordered(stiff_ref[...])).astype(BF16)

    block_at = lax.broadcasted_iota(jnp.int32, (1, total), 1) // edge
    mask = jnp.where(block_at == LEFT, has_left, jnp.where(block_at == RIGHT, has_right, 1.0))

    def start_sides(step, field):
        for k in range(4):
            side_out[step, k] = field[:, k * edge : (k + 1) * edge]
        plan = [
            (LEFT, RIGHT, (left, row)),
            (RIGHT, LEFT, (right, row)),
            (LOWER, UPPER, (col, below)),
            (UPPER, LOWER, (col, above)),
        ]
        return [
            send(
                side_out.at[step, k],
                side_in.at[step, there],
                side_send.at[step, k],
                side_recv.at[step, there],
                device,
            )
            for k, there, device in plan
        ]

    def end_sides(step, field, copies):
        for copy in copies:
            copy.wait_recv()
        arrived = jnp.concatenate([side_in[step, k] for k in range(4)], axis=1)
        return (field + arrived) * mask

    x_rhs = jnp.concatenate(
        [first_in[0, :loads] * has_left, own_right, first_in[1, :loads], own_up], axis=1
    )
    field = wide_dot(x_rhs, stiff_ref[...])
    copies = start_sides(0, field)

    for copy in fetch_z:
        copy.wait_recv()
    for k in range(n_y):
        target = k * line + z
        behind = (target + n_wide - 1) % n_wide
        block_stage[k, 0] = block_z[slot_ref[0, target] % line]
        block_stage[k, 1] = block_z[slot_ref[0, behind] % line]
    fetch_y = [
        send(
            block_stage.at[(y + d + 1) % n_y],
            block_y.at[y],
            block_send.at[1, d],
            block_recv.at[1, d],
            (c, row),
        )
        for d, c in enumerate(along_y)
    ]
    block_y[y] = block_stage[y]

    loading[2].wait()
    basis_ref[...] = jnp.dot(perm, basis_ref[...], preferred_element_type=F32).astype(BF16)
    loading[1].wait()
    greens_ref[...] = reordered(greens_ref[...]).astype(BF16)

    x_z = end_sides(0, field, copies)

    def start_corners(step, part):
        width = part.shape[1] // 4
        for k in range(4):
            corner_out[step, k] = packed(part[:, k * width : (k + 1) * width])
        out = corner_out.at[step]
        plan = [
            (out.at[LL], horiz_in.at[step, LR], (left, row)),
            (out.at[LR], horiz_in.at[step, LL], (right, row)),
            (out.at[UL], horiz_in.at[step, UR], (left, row)),
            (out.at[UR], horiz_in.at[step, UL], (right, row)),
            (out.at[LL], diag_in.at[step, UR], (left, below)),
            (out.at[LR], diag_in.at[step, UL], (right, below)),
            (out.at[UL], diag_in.at[step, LR], (left, above)),
            (out.at[UR], diag_in.at[step, LL], (right, above)),
            (out.at[pl.ds(LL, 2)], vert_in.at[step, pl.ds(UL, 2)], (col, below)),
            (out.at[pl.ds(UL, 2)], vert_in.at[step, pl.ds(LL, 2)], (col, above)),
        ]
        return [
            send(source, target, corner_send.at[step, k], corner_recv.at[step, k], device)
            for k, (source, target, device) in enumerate(plan)
        ]

    def end_corners(step, coarse, copies):
        for copy in copies:
            copy.wait_recv()
        sums = []
        for k in range(4):
            across = horiz_in[step, k] + diag_in[step, k]
            if k in (LR, UR):
                across = across * has_right
            sums.append(unpacked(corner_out[step, k] + vert_in[step, k] + across))
        values = wide_dot(jnp.concatenate(sums, axis=1), coarse)
        at = lax.broadcasted_iota(jnp.int32, (1, values.shape[1]), 1) // (values.shape[1] // 4)
        return values * jnp.where(at % 2 == 0, has_left, 1.0)

    def corrected(local, values):
        return local + wide_dot(values, basis_ref[...], (((1,), (1,)), ((), ())))

    copies = start_corners(0, wide_dot(x_z, basis_ref[...]))
    local = wide_dot(x_z, greens_ref[...])
    for copy in fetch_y:
        copy.wait_recv()
    block_own[1] = block_y[slot_ref[0, left] // line, 1]
    block_own[2] = block_y[slot_ref[0, col] // line, 0]
    hand_down = send(
        block_own.at[pl.ds(1, 2)], block_up, block_send.at[2, 0], block_recv.at[2, 0], (col, below)
    )
    hand_down.wait_recv()
    quarter = [
        unpacked(block.astype(F32)) for block in (block_own[1], block_own[2], block_up[0], block_up[1])
    ]
    width = quarter[0].shape[0]
    nothing = jnp.zeros((width, width), F32)
    coarse = jnp.concatenate(
        [
            jnp.concatenate([quarter[k] if k == m else nothing for m in range(4)], axis=1)
            for k in range(4)
        ],
        axis=0,
    ).astype(BF16)
    field = corrected(local, end_corners(0, coarse, copies))
    copies = start_sides(1, field)
    x_q = end_sides(1, field, copies)

    field = wide_dot(x_q, stiff_ref[...])
    copies = start_sides(2, field)
    x_u = end_sides(2, field, copies)

    copies = start_corners(1, wide_dot(x_u, basis_ref[...]))
    local = wide_dot(x_u, greens_ref[...])

    def own(x):
        return jnp.concatenate([x[:, edge : 2 * edge], x[:, 3 * edge :]], axis=1)

    r_own, z_own, q_own, u_own = own(x_rhs), own(x_z), own(x_q), own(x_u)

    def inner(a, b):
        return jnp.sum(a * b, axis=1, keepdims=True)

    dots = [inner(r_own, z_own), inner(z_own, q_own), inner(r_own, u_own), inner(q_own, u_own)]
    field = corrected(local, end_corners(1, coarse, copies))
    copies = start_sides(3, field)
    dots += [inner(x_z, field), inner(x_u, field)]

    at = lax.broadcasted_iota(jnp.int32, (loads, edge), 1)
    table = jnp.zeros((loads, edge), F32)
    for k, dot in enumerate(dots):
        table = jnp.where(at == k, dot, table)
    table = jnp.concatenate([table, jnp.zeros((edge - loads, edge), F32)], axis=0)
    value = jnp.transpose(table)[:8]

    stages = [
        (row, n_blk, [(col, r) for r in along_blk]),
        (z, line, [(c, row) for c in along_z]),
        (y, n_y, [(c, row) for c in along_y]),
    ]
    for stage, (me, count, devices) in enumerate(stages):
        sum_out[stage] = value
        group = [
            send(
                sum_out.at[stage],
                sum_in.at[stage, me],
                sum_send.at[stage, d],
                sum_recv.at[stage, d],
                device,
            )
            for d, device in enumerate(devices)
        ]
        sum_in[stage, me] = value
        for copy in group:
            copy.wait_recv()
        value = sum_in[stage, 0]
        for k in range(1, count):
            value = value + sum_in[stage, k]

    used = lax.broadcasted_iota(jnp.int32, value.shape, 1) < loads
    value = jnp.where(used, value, 1.0)
    rz, zq, ru, qu, zv, uv = (value[k : k + 1] for k in range(6))
    alpha = rz / zq
    new = alpha * (alpha * qu - ru)
    grown = 1.0 + new / rz
    energy = grown * grown * zq - alpha * grown * (zv + qu) + alpha * alpha * uv
    second = new / energy
    main = alpha + second * grown
    rest = second * alpha
    at = lax.broadcasted_iota(jnp.int32, (edge, edge), 0)
    factors = jnp.transpose(jnp.where(at == 0, main, rest))
    main, rest = factors[:loads, 0:1], factors[:loads, 1:2]
    mult_ref[...] = main * z_own - rest * u_own
    v_own = own(end_sides(3, field, copies))
    res_ref[...] = r_own - main * q_own + rest * v_own

    for copy in sends:
        copy.wait_send()


def body(
    dual_rhs,
    local_inverse,
    dirichlet,
    coarse_basis,
    coarse_inverse,
    corner_slot,
    side_map,
    edge_flip,
):
    loads, pair = dual_rhs.shape[2:]
    edge = pair // 2
    total = 4 * edge
    corner = coarse_inverse.shape[-1]
    n_wide, n_blk = lax.axis_size("wide"), lax.axis_size("blk")
    line = 8
    n_y = n_wide // line
    most = max(line, n_y, n_blk)
    small = (corner // 2, 2 * corner)
    dma = pltpu.SemaphoreType.DMA
    vmem = pl.BlockSpec(memory_space=pltpu.VMEM)
    smem = pl.BlockSpec(memory_space=pltpu.SMEM)
    anywhere = pl.BlockSpec(memory_space=pl.ANY)
    out = jax.ShapeDtypeStruct((loads, pair), F32)
    multipliers, residual = pl.pallas_call(
        functools.partial(kernel, line),
        out_shape=(out, out),
        in_specs=[smem, smem, vmem, vmem, vmem, anywhere, anywhere, anywhere],
        out_specs=(vmem, vmem),
        scratch_shapes=[
            pltpu.VMEM((total, total), BF16),
            pltpu.VMEM((total, total), BF16),
            pltpu.VMEM((total, 4 * corner), BF16),
            dma((3,)),
            pltpu.VMEM((2, loads + 8, edge), F32),
            pltpu.VMEM((2, loads + 8, edge), F32),
            dma((2,)),
            dma((2,)),
            pltpu.VMEM((4, 4, loads, edge), F32),
            pltpu.VMEM((4, 4, loads, edge), F32),
            dma((4, 4)),
            dma((4, 4)),
            pltpu.VMEM((2, 4, loads // 2, 2 * corner), F32),
            pltpu.VMEM((2, 4, loads // 2, 2 * corner), F32),
            pltpu.VMEM((2, 4, loads // 2, 2 * corner), F32),
            pltpu.VMEM((2, 4, loads // 2, 2 * corner), F32),
            dma((2, 10)),
            dma((2, 10)),
            pltpu.VMEM((line,) + small, BF16),
            pltpu.VMEM((n_y, 2) + small, BF16),
            pltpu.VMEM((n_y, 2) + small, BF16),
            pltpu.VMEM((3,) + small, BF16),
            pltpu.VMEM((2,) + small, BF16),
            dma((3, most)),
            dma((3, most)),
            pltpu.VMEM((3, 8, edge), F32),
            pltpu.VMEM((3, most, 8, edge), F32),
            dma((3, most)),
            dma((3, most)),
        ],
        compiler_params=pltpu.CompilerParams(collective_id=0, has_side_effects=True),
        name="krylov",
    )(
        corner_slot,
        edge_flip[0],
        side_map[0],
        dual_rhs[0, 0],
        coarse_inverse[0, 0],
        dirichlet[0, 0],
        local_inverse[0, 0],
        coarse_basis[0, 0],
    )
    return (multipliers[None, None], residual[None, None])


def solution(mesh):
    in_specs = (
        P("wide", "blk", None, None),
        P("wide", "blk", None, None),
        P("wide", "blk", None, None),
        P("wide", "blk", None, None),
        P("wide", "blk", None, None),
        P("blk", None),
        P("wide", "blk", None),
        P("wide", "blk", None),
    )
    out_specs = (P("wide", "blk", None, None), P("wide", "blk", None, None))
    return jax.shard_map(body, mesh=mesh, in_specs=in_specs, out_specs=out_specs, check_vma=False)
```

```python
import functools

import jax
import jax.numpy as jnp
from jax import lax
from jax.experimental import pallas as pl
from jax.experimental.pallas import tpu as pltpu
from jax.sharding import PartitionSpec as P

MESH = pl.DeviceIdType.MESH
F32 = jnp.float32
BF16 = jnp.bfloat16
LEFT, RIGHT, LOWER, UPPER = range(4)
LL, LR, UL, UR = range(4)


def halves(x):
    hi = x.astype(BF16)
    lo = (x - hi.astype(F32)).astype(BF16)
    return jnp.concatenate([hi, lo], axis=0)


def wide_dot(x, matrix, dims=(((1,), (0,)), ((), ()))):
    rows = x.shape[0]
    both = lax.dot_general(halves(x), matrix, dims, preferred_element_type=F32)
    return both[:rows] + both[rows:]


def packed(block):
    rows = block.shape[0] // 2
    return jnp.concatenate([block[:rows], block[rows:]], axis=1)


def unpacked(block):
    width = block.shape[1] // 2
    return jnp.concatenate([block[:, :width], block[:, width:]], axis=0)


def kernel(
    line,
    slot_ref,
    flip_ref,
    map_hbm,
    rhs_hbm,
    cinv_hbm,
    stiff_hbm,
    greens_hbm,
    basis_hbm,
    mult_ref,
    res_ref,
    map_ref,
    rhs_ref,
    cinv_ref,
    stiff_ref,
    greens_ref,
    basis_ref,
    load_sem,
    first_out,
    first_in,
    first_send,
    first_recv,
    side_out,
    side_in,
    side_send,
    side_recv,
    corner_out,
    horiz_in,
    vert_in,
    diag_in,
    corner_send,
    corner_recv,
    block_z,
    block_stage,
    block_y,
    block_own,
    block_up,
    block_send,
    block_recv,
    sum_out,
    sum_in,
    sum_send,
    sum_recv,
):
    loads = rhs_ref.shape[0]
    edge = rhs_ref.shape[1] // 2
    n_wide = lax.axis_size("wide")
    n_blk = lax.axis_size("blk")
    n_y = n_wide // line
    col = lax.axis_index("wide")
    row = lax.axis_index("blk")
    y, z = col // line, col % line
    right, left = (col + 1) % n_wide, (col + n_wide - 1) % n_wide
    above, below = (row + 1) % n_blk, (row + n_blk - 1) % n_blk

    along_z = [y * line + (z + d) % line for d in range(1, line)]
    along_y = [((y + d) % n_y) * line + z for d in range(1, n_y)]
    along_blk = [(row + d) % n_blk for d in range(1, n_blk)]

    barrier = pltpu.get_barrier_semaphore()
    friends = [(c, row) for c in along_z + along_y + [left, right]]
    friends += [(col, r) for r in along_blk]
    friends += [(c, r) for c in (left, right) for r in (below, above)]
    for friend in friends:
        pl.semaphore_signal(barrier, inc=1, device_id=friend, device_id_type=MESH)
    loading = [
        pltpu.make_async_copy(source, target, load_sem.at[k])
        for k, (source, target) in enumerate(
            [
                (stiff_hbm, stiff_ref),
                (greens_hbm, greens_ref),
                (basis_hbm, basis_ref),
                (rhs_hbm, rhs_ref),
                (cinv_hbm, cinv_ref),
                (map_hbm, map_ref),
            ]
        )
    ]
    for k in (3, 4, 5, 0, 2, 1):
        loading[k].start()

    loading[3].wait()
    loading[4].wait()
    pl.semaphore_wait(barrier, len(friends))

    sends = []

    def send(source, target, send_sem, recv_sem, device):
        copy = pltpu.make_async_remote_copy(
            src_ref=source,
            dst_ref=target,
            send_sem=send_sem,
            recv_sem=recv_sem,
            device_id=device,
            device_id_type=MESH,
        )
        copy.start()
        sends.append(copy)
        return copy

    has_left = jnp.where(col > 0, 1.0, 0.0).astype(F32)
    has_right = jnp.where(col < n_wide - 1, 1.0, 0.0).astype(F32)

    own_right = rhs_ref[:, :edge] * has_right
    own_up = rhs_ref[:, edge:]
    first_out[0, :loads] = own_right
    first_out[1, :loads] = own_up
    for k in range(2):
        flag = flip_ref[0, k].astype(F32)
        first_out[k, loads:] = jnp.full((8, edge), 1.0, F32) * flag
    first = [
        send(first_out.at[k], first_in.at[k], first_send.at[k], first_recv.at[k], device)
        for k, device in enumerate([(right, row), (col, above)])
    ]

    block_own[0] = packed(cinv_ref[...]).astype(BF16)
    fetch_z = [
        send(block_own.at[0], block_z.at[z], block_send.at[0, d], block_recv.at[0, d], (c, row))
        for d, c in enumerate(along_z)
    ]
    block_z[z] = block_own[0]

    loading[5].wait()
    total = 4 * edge
    index = jnp.broadcast_to(map_ref[...], (8, total)).astype(F32)
    lane = lax.broadcasted_iota(jnp.int32, (8, total), 1)
    sign = jnp.where((lane // edge) % 2 == 0, -1.0, 1.0).astype(F32)
    columns = jnp.transpose(jnp.concatenate([index, sign], axis=0))
    index_row = map_ref[...]
    index_col = (columns[:, :1] + 0.5).astype(jnp.int32)
    perm_t = jnp.where(
        lax.broadcasted_iota(jnp.int32, (total, total), 0) == index_row, sign[:1], 0.0
    ).astype(BF16)
    perm = jnp.where(
        lax.broadcasted_iota(jnp.int32, (total, total), 1) == index_col, columns[:, 8:9], 0.0
    ).astype(BF16)

    def reordered(matrix):
        half = jnp.dot(perm, matrix, preferred_element_type=F32).astype(BF16)
        return jnp.dot(half, perm_t, preferred_element_type=F32).astype(BF16)

    loading[0].wait()
    stiff = reordered(0.25 * stiff_ref[...])
    loading[2].wait()
    basis = jnp.dot(perm, basis_ref[...], preferred_element_type=F32).astype(BF16)

    for copy in first:
        copy.wait_recv()
    rows_at = lax.broadcasted_iota(jnp.int32, (edge, edge), 0)
    lanes_at = lax.broadcasted_iota(jnp.int32, (edge, edge), 1)
    keep = jnp.where(rows_at == lanes_at, 1.0, 0.0).astype(F32)
    back = jnp.where(rows_at + lanes_at == edge - 1, 1.0, 0.0).astype(F32)
    turns = [
        (keep + first_in[k, loads : loads + 1] * (back - keep)).astype(BF16) for k in range(2)
    ]

    def turned_rows(matrix):
        blocks = [matrix[k * edge : (k + 1) * edge] for k in range(4)]
        for k, turn in zip((LEFT, LOWER), turns):
            blocks[k] = jnp.dot(turn, blocks[k], preferred_element_type=F32).astype(BF16)
        return jnp.concatenate(blocks, axis=0)

    def turned_columns(matrix):
        blocks = [matrix[:, k * edge : (k + 1) * edge] for k in range(4)]
        for k, turn in zip((LEFT, LOWER), turns):
            blocks[k] = jnp.dot(blocks[k], turn, preferred_element_type=F32).astype(BF16)
        return jnp.concatenate(blocks, axis=1)

    stiff_ref[...] = turned_columns(turned_rows(stiff))

    block_at = lax.broadcasted_iota(jnp.int32, (1, total), 1) // edge
    mask = jnp.where(block_at == LEFT, has_left, jnp.where(block_at == RIGHT, has_right, 1.0))

    def start_sides(step, field):
        for k in range(4):
            side_out[step, k] = field[:, k * edge : (k + 1) * edge]
        plan = [
            (LEFT, RIGHT, (left, row)),
            (RIGHT, LEFT, (right, row)),
            (LOWER, UPPER, (col, below)),
            (UPPER, LOWER, (col, above)),
        ]
        return [
            send(
                side_out.at[step, k],
                side_in.at[step, there],
                side_send.at[step, k],
                side_recv.at[step, there],
                device,
            )
            for k, there, device in plan
        ]

    def end_sides(step, field, copies):
        for copy in copies:
            copy.wait_recv()
        arrived = jnp.concatenate([side_in[step, k] for k in range(4)], axis=1)
        return (field + arrived) * mask

    x_rhs = jnp.concatenate(
        [first_in[0, :loads] * has_left, own_right, first_in[1, :loads], own_up], axis=1
    )
    field = wide_dot(x_rhs, stiff_ref[...])
    copies = start_sides(0, field)

    for copy in fetch_z:
        copy.wait_recv()
    for k in range(n_y):
        target = k * line + z
        behind = (target + n_wide - 1) % n_wide
        block_stage[k, 0] = block_z[slot_ref[0, target] % line]
        block_stage[k, 1] = block_z[slot_ref[0, behind] % line]
    fetch_y = [
        send(
            block_stage.at[(y + d + 1) % n_y],
            block_y.at[y],
            block_send.at[1, d],
            block_recv.at[1, d],
            (c, row),
        )
        for d, c in enumerate(along_y)
    ]
    block_y[y] = block_stage[y]

    basis_ref[...] = turned_rows(basis)
    loading[1].wait()
    greens_ref[...] = turned_columns(turned_rows(reordered(greens_ref[...])))

    x_z = end_sides(0, field, copies)

    def start_corners(step, part):
        width = part.shape[1] // 4
        for k in range(4):
            corner_out[step, k] = packed(part[:, k * width : (k + 1) * width])
        out = corner_out.at[step]
        plan = [
            (out.at[LL], horiz_in.at[step, LR], (left, row)),
            (out.at[LR], horiz_in.at[step, LL], (right, row)),
            (out.at[UL], horiz_in.at[step, UR], (left, row)),
            (out.at[UR], horiz_in.at[step, UL], (right, row)),
            (out.at[LL], diag_in.at[step, UR], (left, below)),
            (out.at[LR], diag_in.at[step, UL], (right, below)),
            (out.at[UL], diag_in.at[step, LR], (left, above)),
            (out.at[UR], diag_in.at[step, LL], (right, above)),
            (out.at[pl.ds(LL, 2)], vert_in.at[step, pl.ds(UL, 2)], (col, below)),
            (out.at[pl.ds(UL, 2)], vert_in.at[step, pl.ds(LL, 2)], (col, above)),
        ]
        return [
            send(source, target, corner_send.at[step, k], corner_recv.at[step, k], device)
            for k, (source, target, device) in enumerate(plan)
        ]

    def end_corners(step, coarse, copies):
        for copy in copies:
            copy.wait_recv()
        sums = []
        for k in range(4):
            across = horiz_in[step, k] + diag_in[step, k]
            if k in (LR, UR):
                across = across * has_right
            sums.append(unpacked(corner_out[step, k] + vert_in[step, k] + across))
        values = wide_dot(jnp.concatenate(sums, axis=1), coarse)
        width = values.shape[1] // 4
        at = lax.broadcasted_iota(jnp.int32, (1, values.shape[1]), 1) // width
        own_value = values[:, width : 2 * width]
        return values * jnp.where(at % 2 == 0, has_left, 1.0), sums[LR], own_value

    def corrected(local, values):
        return local + wide_dot(values, basis_ref[...], (((1,), (1,)), ((), ())))

    copies = start_corners(0, wide_dot(x_z, basis_ref[...]))
    local = wide_dot(x_z, greens_ref[...])
    for copy in fetch_y:
        copy.wait_recv()
    block_own[1] = block_y[slot_ref[0, left] // line, 1]
    block_own[2] = block_y[slot_ref[0, col] // line, 0]
    hand_down = send(
        block_own.at[pl.ds(1, 2)], block_up, block_send.at[2, 0], block_recv.at[2, 0], (col, below)
    )
    hand_down.wait_recv()
    quarter = [
        unpacked(block.astype(F32)) for block in (block_own[1], block_own[2], block_up[0], block_up[1])
    ]
    width = quarter[0].shape[0]
    nothing = jnp.zeros((width, width), F32)
    coarse = jnp.concatenate(
        [
            jnp.concatenate([quarter[k] if k == m else nothing for m in range(4)], axis=1)
            for k in range(4)
        ],
        axis=0,
    ).astype(BF16)
    values, z_corner, _ = end_corners(0, coarse, copies)
    field = corrected(local, values)
    copies = start_sides(1, field)
    x_q = end_sides(1, field, copies)

    field = wide_dot(x_q, stiff_ref[...])
    copies = start_sides(2, field)
    x_u = end_sides(2, field, copies)

    copies = start_corners(1, wide_dot(x_u, basis_ref[...]))
    local = wide_dot(x_u, greens_ref[...])

    def own(x):
        return jnp.concatenate([x[:, edge : 2 * edge], x[:, 3 * edge :]], axis=1)

    r_own, z_own, q_own, u_own = own(x_rhs), own(x_z), own(x_q), own(x_u)

    def inner(a, b):
        return jnp.sum(a * b, axis=1, keepdims=True)

    dots = [inner(r_own, z_own), inner(z_own, q_own), inner(r_own, u_own), inner(q_own, u_own)]
    local_dots = [inner(x_z, local), inner(x_u, local)]
    values, u_corner, own_value = end_corners(1, coarse, copies)
    dots += [
        dot + inner(corner, own_value) for dot, corner in zip(local_dots, (z_corner, u_corner))
    ]

    at = lax.broadcasted_iota(jnp.int32, (loads, edge), 1)
    table = jnp.zeros((loads, edge), F32)
    for k, dot in enumerate(dots):
        table = jnp.where(at == k, dot, table)
    table = jnp.concatenate([table, jnp.zeros((edge - loads, edge), F32)], axis=0)
    value = jnp.transpose(table)[:8]

    stages = [
        (row, n_blk, [(col, r) for r in along_blk]),
        (z, line, [(c, row) for c in along_z]),
        (y, n_y, [(c, row) for c in along_y]),
    ]
    for stage, (me, count, devices) in enumerate(stages):
        sum_out[stage] = value
        group = [
            send(
                sum_out.at[stage],
                sum_in.at[stage, me],
                sum_send.at[stage, d],
                sum_recv.at[stage, d],
                device,
            )
            for d, device in enumerate(devices)
        ]
        sum_in[stage, me] = value
        if stage == 0:
            field = corrected(local, values)
            copies = start_sides(3, field)
        for copy in group:
            copy.wait_recv()
        value = sum_in[stage, 0]
        for k in range(1, count):
            value = value + sum_in[stage, k]

    used = lax.broadcasted_iota(jnp.int32, value.shape, 1) < loads
    value = jnp.where(used, value, 1.0)
    rz, zq, ru, qu, zv, uv = (value[k : k + 1] for k in range(6))
    alpha = rz / zq
    new = alpha * (alpha * qu - ru)
    grown = 1.0 + new / rz
    energy = grown * grown * zq - alpha * grown * (zv + qu) + alpha * alpha * uv
    second = new / energy
    main = alpha + second * grown
    rest = second * alpha
    at = lax.broadcasted_iota(jnp.int32, (edge, edge), 0)
    factors = jnp.transpose(jnp.where(at == 0, main, rest))
    main, rest = factors[:loads, 0:1], factors[:loads, 1:2]
    mult_ref[...] = main * z_own - rest * u_own
    v_own = own(end_sides(3, field, copies))
    res_ref[...] = r_own - main * q_own + rest * v_own

    for copy in sends:
        copy.wait_send()


def body(
    dual_rhs,
    local_inverse,
    dirichlet,
    coarse_basis,
    coarse_inverse,
    corner_slot,
    side_map,
    edge_flip,
):
    loads, pair = dual_rhs.shape[2:]
    edge = pair // 2
    total = 4 * edge
    corner = coarse_inverse.shape[-1]
    n_wide, n_blk = lax.axis_size("wide"), lax.axis_size("blk")
    line = 8
    n_y = n_wide // line
    most = max(line, n_y, n_blk)
    small = (corner // 2, 2 * corner)
    dma = pltpu.SemaphoreType.DMA
    vmem = pl.BlockSpec(memory_space=pltpu.VMEM)
    smem = pl.BlockSpec(memory_space=pltpu.SMEM)
    anywhere = pl.BlockSpec(memory_space=pl.ANY)
    out = jax.ShapeDtypeStruct((loads, pair), F32)
    multipliers, residual = pl.pallas_call(
        functools.partial(kernel, line),
        out_shape=(out, out),
        in_specs=[smem, smem] + [anywhere] * 6,
        out_specs=(vmem, vmem),
        scratch_shapes=[
            pltpu.VMEM((1, total), jnp.int32),
            pltpu.VMEM((loads, pair), F32),
            pltpu.VMEM((corner, corner), F32),
            pltpu.VMEM((total, total), BF16),
            pltpu.VMEM((total, total), BF16),
            pltpu.VMEM((total, 4 * corner), BF16),
            dma((6,)),
            pltpu.VMEM((2, loads + 8, edge), F32),
            pltpu.VMEM((2, loads + 8, edge), F32),
            dma((2,)),
            dma((2,)),
            pltpu.VMEM((4, 4, loads, edge), F32),
            pltpu.VMEM((4, 4, loads, edge), F32),
            dma((4, 4)),
            dma((4, 4)),
            pltpu.VMEM((2, 4, loads // 2, 2 * corner), F32),
            pltpu.VMEM((2, 4, loads // 2, 2 * corner), F32),
            pltpu.VMEM((2, 4, loads // 2, 2 * corner), F32),
            pltpu.VMEM((2, 4, loads // 2, 2 * corner), F32),
            dma((2, 10)),
            dma((2, 10)),
            pltpu.VMEM((line,) + small, BF16),
            pltpu.VMEM((n_y, 2) + small, BF16),
            pltpu.VMEM((n_y, 2) + small, BF16),
            pltpu.VMEM((3,) + small, BF16),
            pltpu.VMEM((2,) + small, BF16),
            dma((3, most)),
            dma((3, most)),
            pltpu.VMEM((3, 8, edge), F32),
            pltpu.VMEM((3, most, 8, edge), F32),
            dma((3, most)),
            dma((3, most)),
        ],
        compiler_params=pltpu.CompilerParams(collective_id=0, has_side_effects=True),
        name="krylov",
    )(
        corner_slot,
        edge_flip[0],
        side_map[0],
        dual_rhs[0, 0],
        coarse_inverse[0, 0],
        dirichlet[0, 0],
        local_inverse[0, 0],
        coarse_basis[0, 0],
    )
    return (multipliers[None, None], residual[None, None])


def solution(mesh):
    in_specs = (
        P("wide", "blk", None, None),
        P("wide", "blk", None, None),
        P("wide", "blk", None, None),
        P("wide", "blk", None, None),
        P("wide", "blk", None, None),
        P("blk", None),
        P("wide", "blk", None),
        P("wide", "blk", None),
    )
    out_specs = (P("wide", "blk", None, None), P("wide", "blk", None, None))
    return jax.shard_map(body, mesh=mesh, in_specs=in_specs, out_specs=out_specs, check_vma=False)
```

```python
import functools

import jax
import jax.numpy as jnp
from jax import lax
from jax.experimental import pallas as pl
from jax.experimental.pallas import tpu as pltpu
from jax.sharding import PartitionSpec as P

MESH = pl.DeviceIdType.MESH
F32 = jnp.float32
BF16 = jnp.bfloat16
LEFT, RIGHT, LOWER, UPPER = range(4)
LL, LR, UL, UR = range(4)
CORNERS = [(-1, 0), (0, 0), (-1, 1), (0, 1)]
CROSS = [(0, 0), (-1, 0), (1, 0), (0, -1), (0, 1)]


def moved(step, by):
    return (step[0] + by[0], step[1] + by[1])


REACHED = sorted({moved(patch, corner) for patch in CROSS for corner in CORNERS})
PARTNERS = []
for _a in range(-2, 3):
    for _b in range(-2, 3):
        _shared = [k for k in range(4) if moved((_a, _b), CORNERS[k]) in REACHED]
        if (_a, _b) != (0, 0) and _shared:
            PARTNERS.append(((_a, _b), _shared))
PARTNERS.sort(key=lambda entry: -abs(entry[0][0]) - abs(entry[0][1]))


def halves(x):
    hi = x.astype(BF16)
    lo = (x - hi.astype(F32)).astype(BF16)
    return jnp.concatenate([hi, lo], axis=0)


def wide_dot(x, matrix, dims=(((1,), (0,)), ((), ()))):
    rows = x.shape[0]
    both = lax.dot_general(halves(x), matrix, dims, preferred_element_type=F32)
    return both[:rows] + both[rows:]


def packed(block):
    rows = block.shape[0] // 2
    return jnp.concatenate([block[:rows], block[rows:]], axis=1)


def unpacked(block):
    width = block.shape[1] // 2
    return jnp.concatenate([block[:, :width], block[:, width:]], axis=0)


def kernel(
    line,
    slot_ref,
    flip_ref,
    map_hbm,
    rhs_hbm,
    cinv_hbm,
    stiff_hbm,
    greens_hbm,
    basis_hbm,
    mult_ref,
    res_ref,
    map_ref,
    rhs_ref,
    cinv_ref,
    stiff_ref,
    greens_ref,
    basis_ref,
    load_sem,
    first_out,
    first_in,
    first_send,
    first_recv,
    side_out,
    side_in,
    side_send,
    side_recv,
    edge_out,
    edge_in,
    edge_send,
    edge_recv,
    corner_out,
    corner_in,
    corner_send,
    corner_recv,
    block_z,
    block_stage,
    block_y,
    block_own,
    block_up,
    block_send,
    block_recv,
    sum_out,
    sum_in,
    sum_send,
    sum_recv,
):
    loads = rhs_ref.shape[0]
    edge = rhs_ref.shape[1] // 2
    n_wide = lax.axis_size("wide")
    n_blk = lax.axis_size("blk")
    n_y = n_wide // line
    col = lax.axis_index("wide")
    row = lax.axis_index("blk")
    y, z = col // line, col % line
    right, left = (col + 1) % n_wide, (col + n_wide - 1) % n_wide
    above, below = (row + 1) % n_blk, (row + n_blk - 1) % n_blk

    along_z = [y * line + (z + d) % line for d in range(1, line)]
    along_y = [((y + d) % n_y) * line + z for d in range(1, n_y)]
    along_blk = [(row + d) % n_blk for d in range(1, n_blk)]

    barrier = pltpu.get_barrier_semaphore()
    friends = [(c, row) for c in along_z + along_y + [left, right]]
    friends += [(col, r) for r in along_blk]
    partner_at = [
        ((col + n_wide + a) % n_wide, (row + n_blk + b) % n_blk) for (a, b), _ in PARTNERS
    ]
    friends += [device for ((a, b), _), device in zip(PARTNERS, partner_at) if a and (b or abs(a) > 1)]
    for friend in friends:
        pl.semaphore_signal(barrier, inc=1, device_id=friend, device_id_type=MESH)
    loading = [
        pltpu.make_async_copy(source, target, load_sem.at[k])
        for k, (source, target) in enumerate(
            [
                (stiff_hbm, stiff_ref),
                (greens_hbm, greens_ref),
                (basis_hbm, basis_ref),
                (rhs_hbm, rhs_ref),
                (cinv_hbm, cinv_ref),
                (map_hbm, map_ref),
            ]
        )
    ]
    for k in (3, 4, 5, 0, 2, 1):
        loading[k].start()

    loading[3].wait()
    loading[4].wait()
    pl.semaphore_wait(barrier, len(friends))

    sends = []

    def send(source, target, send_sem, recv_sem, device):
        copy = pltpu.make_async_remote_copy(
            src_ref=source,
            dst_ref=target,
            send_sem=send_sem,
            recv_sem=recv_sem,
            device_id=device,
            device_id_type=MESH,
        )
        copy.start()
        sends.append(copy)
        return copy

    has_left = jnp.where(col > 0, 1.0, 0.0).astype(F32)
    has_right = jnp.where(col < n_wide - 1, 1.0, 0.0).astype(F32)

    own_right = rhs_ref[:, :edge] * has_right
    own_up = rhs_ref[:, edge:]
    first_out[0, :loads] = own_right
    first_out[1, :loads] = own_up
    for k in range(2):
        flag = flip_ref[0, k].astype(F32)
        first_out[k, loads:] = jnp.full((8, edge), 1.0, F32) * flag
    first = [
        send(first_out.at[k], first_in.at[k], first_send.at[k], first_recv.at[k], device)
        for k, device in enumerate([(right, row), (col, above)])
    ]

    block_own[0] = packed(cinv_ref[...]).astype(BF16)
    fetch_z = [
        send(block_own.at[0], block_z.at[z], block_send.at[0, d], block_recv.at[0, d], (c, row))
        for d, c in enumerate(along_z)
    ]
    block_z[z] = block_own[0]

    loading[5].wait()
    total = 4 * edge
    index = jnp.broadcast_to(map_ref[...], (8, total)).astype(F32)
    lane = lax.broadcasted_iota(jnp.int32, (8, total), 1)
    sign = jnp.where((lane // edge) % 2 == 0, -1.0, 1.0).astype(F32)
    columns = jnp.transpose(jnp.concatenate([index, sign], axis=0))
    index_row = map_ref[...]
    index_col = (columns[:, :1] + 0.5).astype(jnp.int32)
    perm_t = jnp.where(
        lax.broadcasted_iota(jnp.int32, (total, total), 0) == index_row, sign[:1], 0.0
    ).astype(BF16)
    perm = jnp.where(
        lax.broadcasted_iota(jnp.int32, (total, total), 1) == index_col, columns[:, 8:9], 0.0
    ).astype(BF16)

    def reordered(matrix):
        half = jnp.dot(perm, matrix, preferred_element_type=F32).astype(BF16)
        return jnp.dot(half, perm_t, preferred_element_type=F32).astype(BF16)

    loading[2].wait()
    basis = jnp.dot(perm, basis_ref[...], preferred_element_type=F32).astype(BF16)
    for k in range(4):
        edge_out[k] = basis[k * edge : (k + 1) * edge]
    plan = [
        (LEFT, RIGHT, (left, row)),
        (RIGHT, LEFT, (right, row)),
        (LOWER, UPPER, (col, below)),
        (UPPER, LOWER, (col, above)),
    ]
    fetch_edges = [
        send(edge_out.at[k], edge_in.at[there], edge_send.at[k], edge_recv.at[there], device)
        for k, there, device in plan
    ]
    loading[0].wait()
    stiff = reordered(0.25 * stiff_ref[...])

    for copy in first:
        copy.wait_recv()
    rows_at = lax.broadcasted_iota(jnp.int32, (edge, edge), 0)
    lanes_at = lax.broadcasted_iota(jnp.int32, (edge, edge), 1)
    keep = jnp.where(rows_at == lanes_at, 1.0, 0.0).astype(F32)
    back = jnp.where(rows_at + lanes_at == edge - 1, 1.0, 0.0).astype(F32)
    turns = [
        (keep + first_in[k, loads : loads + 1] * (back - keep)).astype(BF16) for k in range(2)
    ]

    def turned_rows(matrix):
        blocks = [matrix[k * edge : (k + 1) * edge] for k in range(4)]
        for k, turn in zip((LEFT, LOWER), turns):
            blocks[k] = jnp.dot(turn, blocks[k], preferred_element_type=F32).astype(BF16)
        return jnp.concatenate(blocks, axis=0)

    def turned_columns(matrix):
        blocks = [matrix[:, k * edge : (k + 1) * edge] for k in range(4)]
        for k, turn in zip((LEFT, LOWER), turns):
            blocks[k] = jnp.dot(blocks[k], turn, preferred_element_type=F32).astype(BF16)
        return jnp.concatenate(blocks, axis=1)

    stiff_ref[...] = turned_columns(turned_rows(stiff))

    block_at = lax.broadcasted_iota(jnp.int32, (1, total), 1) // edge
    mask = jnp.where(block_at == LEFT, has_left, jnp.where(block_at == RIGHT, has_right, 1.0))

    def start_sides(step, field):
        for k in range(4):
            side_out[step, k] = field[:, k * edge : (k + 1) * edge]
        return [
            send(
                side_out.at[step, k],
                side_in.at[step, there],
                side_send.at[step, k],
                side_recv.at[step, there],
                device,
            )
            for k, there, device in plan
        ]

    def end_sides(step, field, copies):
        for copy in copies:
            copy.wait_recv()
        arrived = jnp.concatenate([side_in[step, k] for k in range(4)], axis=1)
        return (field + arrived) * mask

    x_rhs = jnp.concatenate(
        [first_in[0, :loads] * has_left, own_right, first_in[1, :loads], own_up], axis=1
    )
    field = wide_dot(x_rhs, stiff_ref[...])
    copies = start_sides(0, field)

    for copy in fetch_z:
        copy.wait_recv()
    for k in range(n_y):
        target = k * line + z
        behind = (target + n_wide - 1) % n_wide
        block_stage[k, 0] = block_z[slot_ref[0, target] % line]
        block_stage[k, 1] = block_z[slot_ref[0, behind] % line]
    fetch_y = [
        send(
            block_stage.at[(y + d + 1) % n_y],
            block_y.at[y],
            block_send.at[1, d],
            block_recv.at[1, d],
            (c, row),
        )
        for d, c in enumerate(along_y)
    ]
    block_y[y] = block_stage[y]

    basis_ref[...] = turned_rows(basis)
    for copy in fetch_edges:
        copy.wait_recv()
    across = [edge_in[k] for k in range(4)]
    for k, side in enumerate((RIGHT, UPPER)):
        own_turn = (keep + flip_ref[0, k].astype(F32) * (back - keep)).astype(BF16)
        across[side] = jnp.dot(own_turn, across[side], preferred_element_type=F32).astype(BF16)
    beyond = jnp.where(col > 1, 1.0, 0.0).astype(F32)

    def start_corners(step, field):
        field = field * mask
        shares = [wide_dot(field, basis_ref[...])] + [
            wide_dot(field[:, k * edge : (k + 1) * edge], across[k]) for k in range(4)
        ]
        reached = {}
        for patch, share in zip(CROSS, shares):
            width = share.shape[1] // 4
            for k in range(4):
                place = moved(patch, CORNERS[k])
                block = packed(share[:, k * width : (k + 1) * width])
                reached[place] = reached[place] + block if place in reached else block
        for place in REACHED:
            if place[0] < 0:
                reached[place] = reached[place] * (has_left if place[0] == -1 else beyond)
        copies = []
        for m, ((steps, shared), device) in enumerate(zip(PARTNERS, partner_at)):
            for n, k in enumerate(shared):
                corner_out[step, m, n] = reached[moved(steps, CORNERS[k])]
            copies.append(
                send(
                    corner_out.at[step, m, pl.ds(0, len(shared))],
                    corner_in.at[step, m, pl.ds(0, len(shared))],
                    corner_send.at[step, m],
                    corner_recv.at[step, m],
                    device,
                )
            )
        return copies, [reached[place] for place in CORNERS]

    def end_corners(step, coarse, copies, sums):
        for copy in copies:
            copy.wait_recv()
        sums = list(sums)
        for m, (_, shared) in enumerate(PARTNERS):
            for n, k in enumerate(shared):
                sums[k] = sums[k] + corner_in[step, m, n]
        sums = [unpacked(block) for block in sums]
        values = wide_dot(jnp.concatenate(sums, axis=1), coarse)
        width = values.shape[1] // 4
        at = lax.broadcasted_iota(jnp.int32, (1, values.shape[1]), 1) // width
        own_value = values[:, width : 2 * width]
        return values * jnp.where(at % 2 == 0, has_left, 1.0), sums[LR], own_value

    def corrected(local, values):
        return local + wide_dot(values, basis_ref[...], (((1,), (1,)), ((), ())))

    corner_copies, sums = start_corners(0, field)
    loading[1].wait()
    greens_ref[...] = turned_columns(turned_rows(reordered(greens_ref[...])))
    x_z = end_sides(0, field, copies)
    local = wide_dot(x_z, greens_ref[...])
    for copy in fetch_y:
        copy.wait_recv()
    block_own[1] = block_y[slot_ref[0, left] // line, 1]
    block_own[2] = block_y[slot_ref[0, col] // line, 0]
    hand_down = send(
        block_own.at[pl.ds(1, 2)], block_up, block_send.at[2, 0], block_recv.at[2, 0], (col, below)
    )
    hand_down.wait_recv()
    quarter = [
        unpacked(block.astype(F32)) for block in (block_own[1], block_own[2], block_up[0], block_up[1])
    ]
    width = quarter[0].shape[0]
    nothing = jnp.zeros((width, width), F32)
    coarse = jnp.concatenate(
        [
            jnp.concatenate([quarter[k] if k == m else nothing for m in range(4)], axis=1)
            for k in range(4)
        ],
        axis=0,
    ).astype(BF16)
    values, z_corner, _ = end_corners(0, coarse, corner_copies, sums)
    field = corrected(local, values)
    copies = start_sides(1, field)
    x_q = end_sides(1, field, copies)

    field = wide_dot(x_q, stiff_ref[...])
    corner_copies, sums = start_corners(1, field)
    copies = start_sides(2, field)
    x_u = end_sides(2, field, copies)

    local = wide_dot(x_u, greens_ref[...])

    def own(x):
        return jnp.concatenate([x[:, edge : 2 * edge], x[:, 3 * edge :]], axis=1)

    r_own, z_own, q_own, u_own = own(x_rhs), own(x_z), own(x_q), own(x_u)

    def inner(a, b):
        return jnp.sum(a * b, axis=1, keepdims=True)

    dots = [inner(r_own, z_own), inner(z_own, q_own), inner(r_own, u_own), inner(q_own, u_own)]
    local_dots = [inner(x_z, local), inner(x_u, local)]
    values, u_corner, own_value = end_corners(1, coarse, corner_copies, sums)
    dots += [
        dot + inner(corner, own_value) for dot, corner in zip(local_dots, (z_corner, u_corner))
    ]

    at = lax.broadcasted_iota(jnp.int32, (loads, edge), 1)
    table = jnp.zeros((loads, edge), F32)
    for k, dot in enumerate(dots):
        table = jnp.where(at == k, dot, table)
    table = jnp.concatenate([table, jnp.zeros((edge - loads, edge), F32)], axis=0)
    value = jnp.transpose(table)[:8]

    stages = [
        (row, n_blk, [(col, r) for r in along_blk]),
        (z, line, [(c, row) for c in along_z]),
        (y, n_y, [(c, row) for c in along_y]),
    ]
    for stage, (me, count, devices) in enumerate(stages):
        sum_out[stage] = value
        group = [
            send(
                sum_out.at[stage],
                sum_in.at[stage, me],
                sum_send.at[stage, d],
                sum_recv.at[stage, d],
                device,
            )
            for d, device in enumerate(devices)
        ]
        sum_in[stage, me] = value
        if stage == 0:
            field = corrected(local, values)
            copies = start_sides(3, field)
        for copy in group:
            copy.wait_recv()
        value = sum_in[stage, 0]
        for k in range(1, count):
            value = value + sum_in[stage, k]

    used = lax.broadcasted_iota(jnp.int32, value.shape, 1) < loads
    value = jnp.where(used, value, 1.0)
    rz, zq, ru, qu, zv, uv = (value[k : k + 1] for k in range(6))
    alpha = rz / zq
    new = alpha * (alpha * qu - ru)
    grown = 1.0 + new / rz
    energy = grown * grown * zq - alpha * grown * (zv + qu) + alpha * alpha * uv
    second = new / energy
    main = alpha + second * grown
    rest = second * alpha
    at = lax.broadcasted_iota(jnp.int32, (edge, edge), 0)
    factors = jnp.transpose(jnp.where(at == 0, main, rest))
    main, rest = factors[:loads, 0:1], factors[:loads, 1:2]
    mult_ref[...] = main * z_own - rest * u_own
    v_own = own(end_sides(3, field, copies))
    res_ref[...] = r_own - main * q_own + rest * v_own

    for copy in sends:
        copy.wait_send()


def body(
    dual_rhs,
    local_inverse,
    dirichlet,
    coarse_basis,
    coarse_inverse,
    corner_slot,
    side_map,
    edge_flip,
):
    loads, pair = dual_rhs.shape[2:]
    edge = pair // 2
    total = 4 * edge
    corner = coarse_inverse.shape[-1]
    n_wide, n_blk = lax.axis_size("wide"), lax.axis_size("blk")
    line = 8
    n_y = n_wide // line
    most = max(line, n_y, n_blk)
    small = (corner // 2, 2 * corner)
    dma = pltpu.SemaphoreType.DMA
    vmem = pl.BlockSpec(memory_space=pltpu.VMEM)
    smem = pl.BlockSpec(memory_space=pltpu.SMEM)
    anywhere = pl.BlockSpec(memory_space=pl.ANY)
    out = jax.ShapeDtypeStruct((loads, pair), F32)
    multipliers, residual = pl.pallas_call(
        functools.partial(kernel, line),
        out_shape=(out, out),
        in_specs=[smem, smem] + [anywhere] * 6,
        out_specs=(vmem, vmem),
        scratch_shapes=[
            pltpu.VMEM((1, total), jnp.int32),
            pltpu.VMEM((loads, pair), F32),
            pltpu.VMEM((corner, corner), F32),
            pltpu.VMEM((total, total), BF16),
            pltpu.VMEM((total, total), BF16),
            pltpu.VMEM((total, 4 * corner), BF16),
            dma((6,)),
            pltpu.VMEM((2, loads + 8, edge), F32),
            pltpu.VMEM((2, loads + 8, edge), F32),
            dma((2,)),
            dma((2,)),
            pltpu.VMEM((4, 4, loads, edge), F32),
            pltpu.VMEM((4, 4, loads, edge), F32),
            dma((4, 4)),
            dma((4, 4)),
            pltpu.VMEM((4, edge, 4 * corner), BF16),
            pltpu.VMEM((4, edge, 4 * corner), BF16),
            dma((4,)),
            dma((4,)),
            pltpu.VMEM((2, len(PARTNERS), 4, loads // 2, 2 * corner), F32),
            pltpu.VMEM((2, len(PARTNERS), 4, loads // 2, 2 * corner), F32),
            dma((2, len(PARTNERS))),
            dma((2, len(PARTNERS))),
            pltpu.VMEM((line,) + small, BF16),
            pltpu.VMEM((n_y, 2) + small, BF16),
            pltpu.VMEM((n_y, 2) + small, BF16),
            pltpu.VMEM((3,) + small, BF16),
            pltpu.VMEM((2,) + small, BF16),
            dma((3, most)),
            dma((3, most)),
            pltpu.VMEM((3, 8, edge), F32),
            pltpu.VMEM((3, most, 8, edge), F32),
            dma((3, most)),
            dma((3, most)),
        ],
        compiler_params=pltpu.CompilerParams(collective_id=0, has_side_effects=True),
        name="krylov",
    )(
        corner_slot,
        edge_flip[0],
        side_map[0],
        dual_rhs[0, 0],
        coarse_inverse[0, 0],
        dirichlet[0, 0],
        local_inverse[0, 0],
        coarse_basis[0, 0],
    )
    return (multipliers[None, None], residual[None, None])


def solution(mesh):
    in_specs = (
        P("wide", "blk", None, None),
        P("wide", "blk", None, None),
        P("wide", "blk", None, None),
        P("wide", "blk", None, None),
        P("wide", "blk", None, None),
        P("blk", None),
        P("wide", "blk", None),
        P("wide", "blk", None),
    )
    out_specs = (P("wide", "blk", None, None), P("wide", "blk", None, None))
    return jax.shard_map(body, mesh=mesh, in_specs=in_specs, out_specs=out_specs, check_vma=False)
```

```python
import functools

import jax
import jax.numpy as jnp
from jax import lax
from jax.experimental import pallas as pl
from jax.experimental.pallas import tpu as pltpu
from jax.sharding import PartitionSpec as P

MESH = pl.DeviceIdType.MESH
F32 = jnp.float32
BF16 = jnp.bfloat16
LEFT, RIGHT, LOWER, UPPER = range(4)
LL, LR, UL, UR = range(4)
CORNERS = [(-1, 0), (0, 0), (-1, 1), (0, 1)]
CROSS = [(0, 0), (-1, 0), (1, 0), (0, -1), (0, 1)]


def moved(step, by):
    return (step[0] + by[0], step[1] + by[1])


REACHED = sorted({moved(patch, corner) for patch in CROSS for corner in CORNERS})
PARTNERS = []
for _a in range(-2, 3):
    for _b in range(-2, 3):
        _shared = [k for k in range(4) if moved((_a, _b), CORNERS[k]) in REACHED]
        if (_a, _b) != (0, 0) and _shared:
            PARTNERS.append(((_a, _b), _shared))
PARTNERS.sort(key=lambda entry: -abs(entry[0][0]) - abs(entry[0][1]))


def halves(x):
    hi = x.astype(BF16)
    lo = (x - hi.astype(F32)).astype(BF16)
    return jnp.concatenate([hi, lo], axis=0)


def wide_dot(x, matrix, dims=(((1,), (0,)), ((), ()))):
    rows = x.shape[0]
    both = lax.dot_general(halves(x), matrix, dims, preferred_element_type=F32)
    return both[:rows] + both[rows:]


def packed(block):
    rows = block.shape[0] // 2
    return jnp.concatenate([block[:rows], block[rows:]], axis=1)


def unpacked(block):
    width = block.shape[1] // 2
    return jnp.concatenate([block[:, :width], block[:, width:]], axis=0)


def kernel(
    line,
    slot_ref,
    flip_ref,
    map_hbm,
    rhs_hbm,
    cinv_hbm,
    stiff_hbm,
    greens_hbm,
    basis_hbm,
    mult_ref,
    res_ref,
    map_ref,
    rhs_ref,
    cinv_ref,
    stiff_ref,
    greens_ref,
    basis_ref,
    load_sem,
    first_out,
    first_in,
    first_send,
    first_recv,
    side_out,
    side_in,
    side_send,
    side_recv,
    edge_out,
    edge_in,
    edge_send,
    edge_recv,
    corner_out,
    corner_in,
    corner_send,
    corner_recv,
    block_z,
    block_stage,
    block_y,
    block_own,
    block_up,
    block_send,
    block_recv,
    sum_out,
    sum_in,
    sum_send,
    sum_recv,
):
    loads = rhs_ref.shape[0]
    edge = rhs_ref.shape[1] // 2
    n_wide = lax.axis_size("wide")
    n_blk = lax.axis_size("blk")
    n_y = n_wide // line
    col = lax.axis_index("wide")
    row = lax.axis_index("blk")
    y, z = col // line, col % line
    right, left = (col + 1) % n_wide, (col + n_wide - 1) % n_wide
    above, below = (row + 1) % n_blk, (row + n_blk - 1) % n_blk

    along_z = [y * line + (z + d) % line for d in range(1, line)]
    along_y = [((y + d) % n_y) * line + z for d in range(1, n_y)]
    along_blk = [(row + d) % n_blk for d in range(1, n_blk)]

    barrier = pltpu.get_barrier_semaphore()
    friends = [(c, row) for c in along_z + along_y + [left, right]]
    friends += [(col, r) for r in along_blk]
    partner_at = [
        ((col + n_wide + a) % n_wide, (row + n_blk + b) % n_blk) for (a, b), _ in PARTNERS
    ]
    friends += [device for ((a, b), _), device in zip(PARTNERS, partner_at) if a and (b or abs(a) > 1)]
    for friend in friends:
        pl.semaphore_signal(barrier, inc=1, device_id=friend, device_id_type=MESH)
    loading = [
        pltpu.make_async_copy(source, target, load_sem.at[k])
        for k, (source, target) in enumerate(
            [
                (stiff_hbm, stiff_ref),
                (greens_hbm, greens_ref),
                (basis_hbm, basis_ref),
                (rhs_hbm, rhs_ref),
                (cinv_hbm, cinv_ref),
                (map_hbm, map_ref),
            ]
        )
    ]
    for k in (3, 4, 5, 0, 2, 1):
        loading[k].start()

    loading[3].wait()
    loading[4].wait()
    pl.semaphore_wait(barrier, len(friends))

    sends = []

    def send(source, target, send_sem, recv_sem, device):
        copy = pltpu.make_async_remote_copy(
            src_ref=source,
            dst_ref=target,
            send_sem=send_sem,
            recv_sem=recv_sem,
            device_id=device,
            device_id_type=MESH,
        )
        copy.start()
        sends.append(copy)
        return copy

    has_left = jnp.where(col > 0, 1.0, 0.0).astype(F32)
    has_right = jnp.where(col < n_wide - 1, 1.0, 0.0).astype(F32)

    own_right = rhs_ref[:, :edge] * has_right
    own_up = rhs_ref[:, edge:]
    first_out[0, :loads] = own_right
    first_out[1, :loads] = own_up
    for k in range(2):
        flag = flip_ref[0, k].astype(F32)
        first_out[k, loads:] = jnp.full((8, edge), 1.0, F32) * flag
    first = [
        send(first_out.at[k], first_in.at[k], first_send.at[k], first_recv.at[k], device)
        for k, device in enumerate([(right, row), (col, above)])
    ]

    block_own[0] = packed(cinv_ref[...]).astype(BF16)
    fetch_z = [
        send(block_own.at[0], block_z.at[z], block_send.at[0, d], block_recv.at[0, d], (c, row))
        for d, c in enumerate(along_z)
    ]
    block_z[z] = block_own[0]

    loading[5].wait()
    total = 4 * edge
    index = jnp.broadcast_to(map_ref[...], (8, total)).astype(F32)
    lane = lax.broadcasted_iota(jnp.int32, (8, total), 1)
    sign = jnp.where((lane // edge) % 2 == 0, -1.0, 1.0).astype(F32)
    columns = jnp.transpose(jnp.concatenate([index, sign], axis=0))
    index_row = map_ref[...]
    index_col = (columns[:, :1] + 0.5).astype(jnp.int32)
    perm_t = jnp.where(
        lax.broadcasted_iota(jnp.int32, (total, total), 0) == index_row, sign[:1], 0.0
    ).astype(BF16)
    perm = jnp.where(
        lax.broadcasted_iota(jnp.int32, (total, total), 1) == index_col, columns[:, 8:9], 0.0
    ).astype(BF16)

    def reordered(matrix):
        half = jnp.dot(perm, matrix, preferred_element_type=F32).astype(BF16)
        return jnp.dot(half, perm_t, preferred_element_type=F32).astype(BF16)

    loading[2].wait()
    basis = jnp.dot(perm, basis_ref[...], preferred_element_type=F32).astype(BF16)
    for k in range(4):
        edge_out[k] = basis[k * edge : (k + 1) * edge]
    plan = [
        (LEFT, RIGHT, (left, row)),
        (RIGHT, LEFT, (right, row)),
        (LOWER, UPPER, (col, below)),
        (UPPER, LOWER, (col, above)),
    ]
    fetch_edges = [
        send(edge_out.at[k], edge_in.at[there], edge_send.at[k], edge_recv.at[there], device)
        for k, there, device in plan
    ]
    loading[0].wait()
    stiff = reordered(0.25 * stiff_ref[...])

    for copy in first:
        copy.wait_recv()
    rows_at = lax.broadcasted_iota(jnp.int32, (edge, edge), 0)
    lanes_at = lax.broadcasted_iota(jnp.int32, (edge, edge), 1)
    keep = jnp.where(rows_at == lanes_at, 1.0, 0.0).astype(F32)
    back = jnp.where(rows_at + lanes_at == edge - 1, 1.0, 0.0).astype(F32)
    turns = [
        (keep + first_in[k, loads : loads + 1] * (back - keep)).astype(BF16) for k in range(2)
    ]

    def turned_rows(matrix):
        blocks = [matrix[k * edge : (k + 1) * edge] for k in range(4)]
        for k, turn in zip((LEFT, LOWER), turns):
            blocks[k] = jnp.dot(turn, blocks[k], preferred_element_type=F32).astype(BF16)
        return jnp.concatenate(blocks, axis=0)

    def turned_columns(matrix):
        blocks = [matrix[:, k * edge : (k + 1) * edge] for k in range(4)]
        for k, turn in zip((LEFT, LOWER), turns):
            blocks[k] = jnp.dot(blocks[k], turn, preferred_element_type=F32).astype(BF16)
        return jnp.concatenate(blocks, axis=1)

    stiff_ref[...] = turned_columns(turned_rows(stiff))

    block_at = lax.broadcasted_iota(jnp.int32, (1, total), 1) // edge
    mask = jnp.where(block_at == LEFT, has_left, jnp.where(block_at == RIGHT, has_right, 1.0))

    def start_sides(step, field):
        for k in range(4):
            side_out[step, k] = field[:, k * edge : (k + 1) * edge]
        return [
            send(
                side_out.at[step, k],
                side_in.at[step, there],
                side_send.at[step, k],
                side_recv.at[step, there],
                device,
            )
            for k, there, device in plan
        ]

    def end_sides(step, field, copies):
        for copy in copies:
            copy.wait_recv()
        arrived = jnp.concatenate([side_in[step, k] for k in range(4)], axis=1)
        return (field + arrived) * mask

    x_rhs = jnp.concatenate(
        [first_in[0, :loads] * has_left, own_right, first_in[1, :loads], own_up], axis=1
    )
    field = wide_dot(x_rhs, stiff_ref[...])
    copies = start_sides(0, field)

    for copy in fetch_z:
        copy.wait_recv()
    for k in range(n_y):
        target = k * line + z
        behind = (target + n_wide - 1) % n_wide
        block_stage[k, 0] = block_z[slot_ref[0, target] % line]
        block_stage[k, 1] = block_z[slot_ref[0, behind] % line]
    fetch_y = [
        send(
            block_stage.at[(y + d + 1) % n_y],
            block_y.at[y],
            block_send.at[1, d],
            block_recv.at[1, d],
            (c, row),
        )
        for d, c in enumerate(along_y)
    ]
    block_y[y] = block_stage[y]

    basis_ref[...] = turned_rows(basis)
    for copy in fetch_edges:
        copy.wait_recv()
    across = [edge_in[k] for k in range(4)]
    for k, side in enumerate((RIGHT, UPPER)):
        own_turn = (keep + flip_ref[0, k].astype(F32) * (back - keep)).astype(BF16)
        across[side] = jnp.dot(own_turn, across[side], preferred_element_type=F32).astype(BF16)
    beyond = jnp.where(col > 1, 1.0, 0.0).astype(F32)

    def start_corners(step, field):
        field = field * mask
        shares = [wide_dot(field, basis_ref[...])] + [
            wide_dot(field[:, k * edge : (k + 1) * edge], across[k]) for k in range(4)
        ]
        reached = {}
        for patch, share in zip(CROSS, shares):
            width = share.shape[1] // 4
            for k in range(4):
                place = moved(patch, CORNERS[k])
                block = packed(share[:, k * width : (k + 1) * width])
                reached[place] = reached[place] + block if place in reached else block
        for place in REACHED:
            if place[0] < 0:
                reached[place] = reached[place] * (has_left if place[0] == -1 else beyond)
        copies = []
        for m, ((steps, shared), device) in enumerate(zip(PARTNERS, partner_at)):
            for n, k in enumerate(shared):
                corner_out[step, m, n] = reached[moved(steps, CORNERS[k])].astype(BF16)
            copies.append(
                send(
                    corner_out.at[step, m, pl.ds(0, len(shared))],
                    corner_in.at[step, m, pl.ds(0, len(shared))],
                    corner_send.at[step, m],
                    corner_recv.at[step, m],
                    device,
                )
            )
        return copies, [reached[place] for place in CORNERS]

    def end_corners(step, coarse, copies, sums):
        for copy in copies:
            copy.wait_recv()
        sums = list(sums)
        for m, (_, shared) in enumerate(PARTNERS):
            for n, k in enumerate(shared):
                sums[k] = sums[k] + corner_in[step, m, n].astype(F32)
        sums = [unpacked(block) for block in sums]
        values = wide_dot(jnp.concatenate(sums, axis=1), coarse)
        width = values.shape[1] // 4
        at = lax.broadcasted_iota(jnp.int32, (1, values.shape[1]), 1) // width
        own_value = values[:, width : 2 * width]
        return values * jnp.where(at % 2 == 0, has_left, 1.0), sums[LR], own_value

    def corrected(local, values):
        return local + wide_dot(values, basis_ref[...], (((1,), (1,)), ((), ())))

    corner_copies, sums = start_corners(0, field)
    loading[1].wait()
    greens_ref[...] = turned_columns(turned_rows(reordered(greens_ref[...])))
    x_z = end_sides(0, field, copies)
    local = wide_dot(x_z, greens_ref[...])
    for copy in fetch_y:
        copy.wait_recv()
    block_own[1] = block_y[slot_ref[0, left] // line, 1]
    block_own[2] = block_y[slot_ref[0, col] // line, 0]
    hand_down = send(
        block_own.at[pl.ds(1, 2)], block_up, block_send.at[2, 0], block_recv.at[2, 0], (col, below)
    )
    hand_down.wait_recv()
    quarter = [
        unpacked(block.astype(F32)) for block in (block_own[1], block_own[2], block_up[0], block_up[1])
    ]
    width = quarter[0].shape[0]
    nothing = jnp.zeros((width, width), F32)
    coarse = jnp.concatenate(
        [
            jnp.concatenate([quarter[k] if k == m else nothing for m in range(4)], axis=1)
            for k in range(4)
        ],
        axis=0,
    ).astype(BF16)
    values, z_corner, _ = end_corners(0, coarse, corner_copies, sums)
    field = corrected(local, values)
    copies = start_sides(1, field)
    x_q = end_sides(1, field, copies)

    field = wide_dot(x_q, stiff_ref[...])
    corner_copies, sums = start_corners(1, field)
    copies = start_sides(2, field)
    x_u = end_sides(2, field, copies)

    local = wide_dot(x_u, greens_ref[...])

    def own(x):
        return jnp.concatenate([x[:, edge : 2 * edge], x[:, 3 * edge :]], axis=1)

    r_own, z_own, q_own, u_own = own(x_rhs), own(x_z), own(x_q), own(x_u)

    def inner(a, b):
        return jnp.sum(a * b, axis=1, keepdims=True)

    dots = [inner(r_own, z_own), inner(z_own, q_own), inner(r_own, u_own), inner(q_own, u_own)]
    local_dots = [inner(x_z, local), inner(x_u, local)]
    values, u_corner, own_value = end_corners(1, coarse, corner_copies, sums)
    dots += [
        dot + inner(corner, own_value) for dot, corner in zip(local_dots, (z_corner, u_corner))
    ]

    at = lax.broadcasted_iota(jnp.int32, (loads, edge), 1)
    table = jnp.zeros((loads, edge), F32)
    for k, dot in enumerate(dots):
        table = jnp.where(at == k, dot, table)
    table = jnp.concatenate([table, jnp.zeros((edge - loads, edge), F32)], axis=0)
    value = jnp.transpose(table)[:8]

    stages = [
        (row, n_blk, [(col, r) for r in along_blk]),
        (z, line, [(c, row) for c in along_z]),
        (y, n_y, [(c, row) for c in along_y]),
    ]
    for stage, (me, count, devices) in enumerate(stages):
        sum_out[stage] = value
        group = [
            send(
                sum_out.at[stage],
                sum_in.at[stage, me],
                sum_send.at[stage, d],
                sum_recv.at[stage, d],
                device,
            )
            for d, device in enumerate(devices)
        ]
        sum_in[stage, me] = value
        if stage == 0:
            field = corrected(local, values)
            copies = start_sides(3, field)
        for copy in group:
            copy.wait_recv()
        value = sum_in[stage, 0]
        for k in range(1, count):
            value = value + sum_in[stage, k]

    used = lax.broadcasted_iota(jnp.int32, value.shape, 1) < loads
    value = jnp.where(used, value, 1.0)
    rz, zq, ru, qu, zv, uv = (value[k : k + 1] for k in range(6))
    alpha = rz / zq
    new = alpha * (alpha * qu - ru)
    grown = 1.0 + new / rz
    energy = grown * grown * zq - alpha * grown * (zv + qu) + alpha * alpha * uv
    second = new / energy
    main = alpha + second * grown
    rest = second * alpha
    at = lax.broadcasted_iota(jnp.int32, (edge, edge), 0)
    factors = jnp.transpose(jnp.where(at == 0, main, rest))
    main, rest = factors[:loads, 0:1], factors[:loads, 1:2]
    mult_ref[...] = main * z_own - rest * u_own
    v_own = own(end_sides(3, field, copies))
    res_ref[...] = r_own - main * q_own + rest * v_own

    for copy in sends:
        copy.wait_send()


def body(
    dual_rhs,
    local_inverse,
    dirichlet,
    coarse_basis,
    coarse_inverse,
    corner_slot,
    side_map,
    edge_flip,
):
    loads, pair = dual_rhs.shape[2:]
    edge = pair // 2
    total = 4 * edge
    corner = coarse_inverse.shape[-1]
    n_wide, n_blk = lax.axis_size("wide"), lax.axis_size("blk")
    line = 8
    n_y = n_wide // line
    most = max(line, n_y, n_blk)
    small = (corner // 2, 2 * corner)
    dma = pltpu.SemaphoreType.DMA
    vmem = pl.BlockSpec(memory_space=pltpu.VMEM)
    smem = pl.BlockSpec(memory_space=pltpu.SMEM)
    anywhere = pl.BlockSpec(memory_space=pl.ANY)
    out = jax.ShapeDtypeStruct((loads, pair), F32)
    multipliers, residual = pl.pallas_call(
        functools.partial(kernel, line),
        out_shape=(out, out),
        in_specs=[smem, smem] + [anywhere] * 6,
        out_specs=(vmem, vmem),
        scratch_shapes=[
            pltpu.VMEM((1, total), jnp.int32),
            pltpu.VMEM((loads, pair), F32),
            pltpu.VMEM((corner, corner), F32),
            pltpu.VMEM((total, total), BF16),
            pltpu.VMEM((total, total), BF16),
            pltpu.VMEM((total, 4 * corner), BF16),
            dma((6,)),
            pltpu.VMEM((2, loads + 8, edge), F32),
            pltpu.VMEM((2, loads + 8, edge), F32),
            dma((2,)),
            dma((2,)),
            pltpu.VMEM((4, 4, loads, edge), F32),
            pltpu.VMEM((4, 4, loads, edge), F32),
            dma((4, 4)),
            dma((4, 4)),
            pltpu.VMEM((4, edge, 4 * corner), BF16),
            pltpu.VMEM((4, edge, 4 * corner), BF16),
            dma((4,)),
            dma((4,)),
            pltpu.VMEM((2, len(PARTNERS), 4, loads // 2, 2 * corner), BF16),
            pltpu.VMEM((2, len(PARTNERS), 4, loads // 2, 2 * corner), BF16),
            dma((2, len(PARTNERS))),
            dma((2, len(PARTNERS))),
            pltpu.VMEM((line,) + small, BF16),
            pltpu.VMEM((n_y, 2) + small, BF16),
            pltpu.VMEM((n_y, 2) + small, BF16),
            pltpu.VMEM((3,) + small, BF16),
            pltpu.VMEM((2,) + small, BF16),
            dma((3, most)),
            dma((3, most)),
            pltpu.VMEM((3, 8, edge), F32),
            pltpu.VMEM((3, most, 8, edge), F32),
            dma((3, most)),
            dma((3, most)),
        ],
        compiler_params=pltpu.CompilerParams(collective_id=0, has_side_effects=True),
        name="krylov",
    )(
        corner_slot,
        edge_flip[0],
        side_map[0],
        dual_rhs[0, 0],
        coarse_inverse[0, 0],
        dirichlet[0, 0],
        local_inverse[0, 0],
        coarse_basis[0, 0],
    )
    return (multipliers[None, None], residual[None, None])


def solution(mesh):
    in_specs = (
        P("wide", "blk", None, None),
        P("wide", "blk", None, None),
        P("wide", "blk", None, None),
        P("wide", "blk", None, None),
        P("wide", "blk", None, None),
        P("blk", None),
        P("wide", "blk", None),
        P("wide", "blk", None),
    )
    out_specs = (P("wide", "blk", None, None), P("wide", "blk", None, None))
    return jax.shard_map(body, mesh=mesh, in_specs=in_specs, out_specs=out_specs, check_vma=False)
```

```python
import functools

import jax
import jax.numpy as jnp
from jax import lax
from jax.experimental import pallas as pl
from jax.experimental.pallas import tpu as pltpu
from jax.sharding import PartitionSpec as P

MESH = pl.DeviceIdType.MESH
F32 = jnp.float32
BF16 = jnp.bfloat16
LEFT, RIGHT, LOWER, UPPER = range(4)
LL, LR, UL, UR = range(4)
CORNERS = [(-1, 0), (0, 0), (-1, 1), (0, 1)]
CROSS = [(0, 0), (-1, 0), (1, 0), (0, -1), (0, 1)]


def moved(step, by):
    return (step[0] + by[0], step[1] + by[1])


REACHED = sorted({moved(patch, corner) for patch in CROSS for corner in CORNERS})
PARTNERS = []
for _a in range(-2, 3):
    for _b in range(-2, 3):
        _shared = [k for k in range(4) if moved((_a, _b), CORNERS[k]) in REACHED]
        if (_a, _b) != (0, 0) and _shared:
            PARTNERS.append(((_a, _b), sorted(_shared, key=lambda k: k != LR)))
PARTNERS.sort(key=lambda entry: -abs(entry[0][0]) - abs(entry[0][1]))


def halves(x):
    hi = x.astype(BF16)
    lo = (x - hi.astype(F32)).astype(BF16)
    return jnp.concatenate([hi, lo], axis=0)


def wide_dot(x, matrix, dims=(((1,), (0,)), ((), ()))):
    rows = x.shape[0]
    both = lax.dot_general(halves(x), matrix, dims, preferred_element_type=F32)
    return both[:rows] + both[rows:]


def packed(block):
    rows = block.shape[0] // 2
    return jnp.concatenate([block[:rows], block[rows:]], axis=1)


def unpacked(block):
    width = block.shape[1] // 2
    return jnp.concatenate([block[:, :width], block[:, width:]], axis=0)


def kernel(
    line,
    slot_hbm,
    flip_hbm,
    map_hbm,
    rhs_hbm,
    cinv_hbm,
    stiff_hbm,
    greens_hbm,
    basis_hbm,
    mult_ref,
    res_ref,
    slot_ref,
    flip_ref,
    map_ref,
    rhs_ref,
    cinv_ref,
    stiff_ref,
    greens_ref,
    basis_ref,
    load_sem,
    first_out,
    first_in,
    first_send,
    first_recv,
    side_out,
    side_in,
    side_send,
    side_recv,
    edge_out,
    edge_in,
    edge_send,
    edge_recv,
    corner_out,
    corner_in,
    corner_send,
    corner_recv,
    block_z,
    block_stage,
    block_y,
    block_own,
    block_up,
    block_send,
    block_recv,
    sum_out,
    sum_in,
    sum_send,
    sum_recv,
):
    loads = rhs_ref.shape[0]
    edge = rhs_ref.shape[1] // 2
    n_wide = lax.axis_size("wide")
    n_blk = lax.axis_size("blk")
    n_y = n_wide // line
    col = lax.axis_index("wide")
    row = lax.axis_index("blk")
    y, z = col // line, col % line
    right, left = (col + 1) % n_wide, (col + n_wide - 1) % n_wide
    above, below = (row + 1) % n_blk, (row + n_blk - 1) % n_blk

    along_z = [y * line + (z + d) % line for d in range(1, line)]
    along_y = [((y + d) % n_y) * line + z for d in range(1, n_y)]
    along_blk = [(row + d) % n_blk for d in range(1, n_blk)]

    barrier = pltpu.get_barrier_semaphore()
    friends = [(c, row) for c in along_z + along_y + [left, right]]
    friends += [(col, r) for r in along_blk]
    partner_at = [
        ((col + n_wide + a) % n_wide, (row + n_blk + b) % n_blk) for (a, b), _ in PARTNERS
    ]
    friends += [device for ((a, b), _), device in zip(PARTNERS, partner_at) if a and (b or abs(a) > 1)]
    for friend in friends:
        pl.semaphore_signal(barrier, inc=1, device_id=friend, device_id_type=MESH)
    loading = [
        pltpu.make_async_copy(source, target, load_sem.at[k])
        for k, (source, target) in enumerate(
            [
                (stiff_hbm, stiff_ref),
                (greens_hbm, greens_ref),
                (basis_hbm, basis_ref),
                (rhs_hbm, rhs_ref),
                (cinv_hbm, cinv_ref),
                (map_hbm, map_ref),
                (flip_hbm, flip_ref),
                (slot_hbm, slot_ref),
            ]
        )
    ]
    for k in (3, 6, 4, 5, 2, 0, 7, 1):
        loading[k].start()

    loading[3].wait()
    loading[6].wait()
    loading[4].wait()
    pl.semaphore_wait(barrier, len(friends))

    sends = []

    def send(source, target, send_sem, recv_sem, device):
        copy = pltpu.make_async_remote_copy(
            src_ref=source,
            dst_ref=target,
            send_sem=send_sem,
            recv_sem=recv_sem,
            device_id=device,
            device_id_type=MESH,
        )
        copy.start()
        sends.append(copy)
        return copy

    has_left = jnp.where(col > 0, 1.0, 0.0).astype(F32)
    has_right = jnp.where(col < n_wide - 1, 1.0, 0.0).astype(F32)

    own_right = rhs_ref[:, :edge] * has_right
    own_up = rhs_ref[:, edge:]
    first_out[0, :loads] = own_right
    first_out[1, :loads] = own_up
    for k in range(2):
        flag = flip_ref[0, k].astype(F32)
        first_out[k, loads:] = jnp.full((8, edge), 1.0, F32) * flag
    first = [
        send(first_out.at[k], first_in.at[k], first_send.at[k], first_recv.at[k], device)
        for k, device in enumerate([(right, row), (col, above)])
    ]

    block_own[0] = packed(cinv_ref[...]).astype(BF16)
    fetch_z = [
        send(block_own.at[0], block_z.at[z], block_send.at[0, d], block_recv.at[0, d], (c, row))
        for d, c in enumerate(along_z)
    ]
    block_z[z] = block_own[0]

    loading[5].wait()
    total = 4 * edge
    index = jnp.broadcast_to(map_ref[...], (8, total)).astype(F32)
    lane = lax.broadcasted_iota(jnp.int32, (8, total), 1)
    sign = jnp.where((lane // edge) % 2 == 0, -1.0, 1.0).astype(F32)
    columns = jnp.transpose(jnp.concatenate([index, sign], axis=0))
    index_row = map_ref[...]
    index_col = (columns[:, :1] + 0.5).astype(jnp.int32)
    perm_t = jnp.where(
        lax.broadcasted_iota(jnp.int32, (total, total), 0) == index_row, sign[:1], 0.0
    ).astype(BF16)
    perm = jnp.where(
        lax.broadcasted_iota(jnp.int32, (total, total), 1) == index_col, columns[:, 8:9], 0.0
    ).astype(BF16)

    def reordered(matrix):
        half = jnp.dot(perm, matrix, preferred_element_type=F32).astype(BF16)
        return jnp.dot(half, perm_t, preferred_element_type=F32).astype(BF16)

    loading[2].wait()
    basis = jnp.dot(perm, basis_ref[...], preferred_element_type=F32).astype(BF16)
    for k in range(4):
        edge_out[k] = basis[k * edge : (k + 1) * edge]
    plan = [
        (LEFT, RIGHT, (left, row)),
        (RIGHT, LEFT, (right, row)),
        (LOWER, UPPER, (col, below)),
        (UPPER, LOWER, (col, above)),
    ]
    fetch_edges = [
        send(edge_out.at[k], edge_in.at[there], edge_send.at[k], edge_recv.at[there], device)
        for k, there, device in plan
    ]
    loading[0].wait()
    stiff = reordered(0.25 * stiff_ref[...])

    for copy in first:
        copy.wait_recv()
    rows_at = lax.broadcasted_iota(jnp.int32, (edge, edge), 0)
    lanes_at = lax.broadcasted_iota(jnp.int32, (edge, edge), 1)
    keep = jnp.where(rows_at == lanes_at, 1.0, 0.0).astype(F32)
    back = jnp.where(rows_at + lanes_at == edge - 1, 1.0, 0.0).astype(F32)
    turns = [
        (keep + first_in[k, loads : loads + 1] * (back - keep)).astype(BF16) for k in range(2)
    ]

    def turned_rows(matrix):
        blocks = [matrix[k * edge : (k + 1) * edge] for k in range(4)]
        for k, turn in zip((LEFT, LOWER), turns):
            blocks[k] = jnp.dot(turn, blocks[k], preferred_element_type=F32).astype(BF16)
        return jnp.concatenate(blocks, axis=0)

    def turned_columns(matrix):
        blocks = [matrix[:, k * edge : (k + 1) * edge] for k in range(4)]
        for k, turn in zip((LEFT, LOWER), turns):
            blocks[k] = jnp.dot(blocks[k], turn, preferred_element_type=F32).astype(BF16)
        return jnp.concatenate(blocks, axis=1)

    stiff_ref[...] = turned_columns(turned_rows(stiff))

    block_at = lax.broadcasted_iota(jnp.int32, (1, total), 1) // edge
    mask = jnp.where(block_at == LEFT, has_left, jnp.where(block_at == RIGHT, has_right, 1.0))

    def start_sides(step, field):
        for k in range(4):
            side_out[step, k] = field[:, k * edge : (k + 1) * edge]
        return [
            send(
                side_out.at[step, k],
                side_in.at[step, there],
                side_send.at[step, k],
                side_recv.at[step, there],
                device,
            )
            for k, there, device in plan
        ]

    def end_sides(step, field, copies):
        for copy in copies:
            copy.wait_recv()
        arrived = jnp.concatenate([side_in[step, k] for k in range(4)], axis=1)
        return (field + arrived) * mask

    x_rhs = jnp.concatenate(
        [first_in[0, :loads] * has_left, own_right, first_in[1, :loads], own_up], axis=1
    )
    field = wide_dot(x_rhs, stiff_ref[...])
    copies = start_sides(0, field)

    for copy in fetch_z:
        copy.wait_recv()
    loading[7].wait()
    for k in range(n_y):
        target = k * line + z
        behind = (target + n_wide - 1) % n_wide
        block_stage[k, 0] = block_z[slot_ref[0, target] % line]
        block_stage[k, 1] = block_z[slot_ref[0, behind] % line]
    fetch_y = [
        send(
            block_stage.at[(y + d + 1) % n_y],
            block_y.at[y],
            block_send.at[1, d],
            block_recv.at[1, d],
            (c, row),
        )
        for d, c in enumerate(along_y)
    ]
    block_y[y] = block_stage[y]

    basis_ref[...] = turned_rows(basis)
    for copy in fetch_edges:
        copy.wait_recv()
    across = [edge_in[k] for k in range(4)]
    for k, side in enumerate((RIGHT, UPPER)):
        own_turn = (keep + flip_ref[0, k].astype(F32) * (back - keep)).astype(BF16)
        across[side] = jnp.dot(own_turn, across[side], preferred_element_type=F32).astype(BF16)
    beyond = jnp.where(col > 1, 1.0, 0.0).astype(F32)

    def start_corners(step, field, sides=None):
        copies = [], []
        whole, field = field, field * mask
        shares = [wide_dot(field, basis_ref[...])] + [
            wide_dot(field[:, k * edge : (k + 1) * edge], across[k]) for k in range(4)
        ]
        reached = {}
        for patch, share in zip(CROSS, shares):
            width = share.shape[1] // 4
            for k in range(4):
                place = moved(patch, CORNERS[k])
                block = packed(share[:, k * width : (k + 1) * width])
                reached[place] = reached[place] + block if place in reached else block
        for place in REACHED:
            if place[0] < 0:
                reached[place] = reached[place] * (has_left if place[0] == -1 else beyond)
        for m, (steps, shared) in enumerate(PARTNERS):
            for n, k in enumerate(shared):
                corner_out[step, m, n] = reached[moved(steps, CORNERS[k])].astype(BF16)
        for part in range(2):
            if part == 1 and sides is not None:
                sides += start_sides(2, whole)
            for m, ((_, shared), device) in enumerate(zip(PARTNERS, partner_at)):
                ahead = 1 if sides is not None and shared[0] == LR else 0
                first, last = (0, ahead) if part == 0 else (ahead, len(shared))
                if first < last:
                    rows = pl.ds(first, last - first)
                    copies[part].append(
                        send(
                            corner_out.at[step, m, rows],
                            corner_in.at[step, m, rows],
                            corner_send.at[step, part, m],
                            corner_recv.at[step, part, m],
                            device,
                        )
                    )
        return copies, [reached[place] for place in CORNERS]

    def own_corner(step, copies, sums):
        for copy in copies[0]:
            copy.wait_recv()
        total = sums[LR]
        for m, (_, shared) in enumerate(PARTNERS):
            if shared[0] == LR:
                total = total + corner_in[step, m, 0].astype(F32)
        return unpacked(total)

    def end_corners(step, coarse, copies, sums):
        for copy in copies[1]:
            copy.wait_recv()
        sums = list(sums)
        for m, (_, shared) in enumerate(PARTNERS):
            for n, k in enumerate(shared):
                sums[k] = sums[k] + corner_in[step, m, n].astype(F32)
        sums = [unpacked(block) for block in sums]
        values = wide_dot(jnp.concatenate(sums, axis=1), coarse)
        at = lax.broadcasted_iota(jnp.int32, (1, values.shape[1]), 1) // (values.shape[1] // 4)
        return values * jnp.where(at % 2 == 0, has_left, 1.0), sums[LR]

    def corrected(local, values):
        return local + wide_dot(values, basis_ref[...], (((1,), (1,)), ((), ())))

    corner_copies, sums = start_corners(0, field)
    loading[1].wait()
    greens_ref[...] = turned_columns(turned_rows(reordered(greens_ref[...])))
    x_z = end_sides(0, field, copies)
    local = wide_dot(x_z, greens_ref[...])
    for copy in fetch_y:
        copy.wait_recv()
    block_own[1] = block_y[slot_ref[0, left] // line, 1]
    block_own[2] = block_y[slot_ref[0, col] // line, 0]
    hand_down = send(
        block_own.at[pl.ds(1, 2)], block_up, block_send.at[2, 0], block_recv.at[2, 0], (col, below)
    )
    hand_down.wait_recv()
    quarter = [
        unpacked(block.astype(F32)) for block in (block_own[1], block_own[2], block_up[0], block_up[1])
    ]
    width = quarter[0].shape[0]
    nothing = jnp.zeros((width, width), F32)
    coarse = jnp.concatenate(
        [
            jnp.concatenate([quarter[k] if k == m else nothing for m in range(4)], axis=1)
            for k in range(4)
        ],
        axis=0,
    ).astype(BF16)
    values, z_corner = end_corners(0, coarse, corner_copies, sums)
    field = corrected(local, values)
    copies = start_sides(1, field)
    x_q = end_sides(1, field, copies)

    field = wide_dot(x_q, stiff_ref[...])
    copies = []
    corner_copies, sums = start_corners(1, field, copies)
    x_u = end_sides(2, field, copies)

    local = wide_dot(x_u, greens_ref[...])

    def own(x):
        return jnp.concatenate([x[:, edge : 2 * edge], x[:, 3 * edge :]], axis=1)

    r_own, z_own, q_own, u_own = own(x_rhs), own(x_z), own(x_q), own(x_u)

    def inner(a, b):
        return jnp.sum(a * b, axis=1, keepdims=True)

    dots = [inner(r_own, z_own), inner(z_own, q_own), inner(r_own, u_own), inner(q_own, u_own)]
    local_dots = [inner(x_z, local), inner(x_u, local)]
    u_corner = own_corner(1, corner_copies, sums)
    own_value = wide_dot(u_corner, quarter[LR].astype(BF16))
    dots += [
        dot + inner(corner, own_value) for dot, corner in zip(local_dots, (z_corner, u_corner))
    ]

    at = lax.broadcasted_iota(jnp.int32, (loads, edge), 1)
    table = jnp.zeros((loads, edge), F32)
    for k, dot in enumerate(dots):
        table = jnp.where(at == k, dot, table)
    table = jnp.concatenate([table, jnp.zeros((edge - loads, edge), F32)], axis=0)
    value = jnp.transpose(table)[:8]

    stages = [
        (row, n_blk, [(col, r) for r in along_blk]),
        (z, line, [(c, row) for c in along_z]),
        (y, n_y, [(c, row) for c in along_y]),
    ]
    for stage, (me, count, devices) in enumerate(stages):
        sum_out[stage] = value
        group = [
            send(
                sum_out.at[stage],
                sum_in.at[stage, me],
                sum_send.at[stage, d],
                sum_recv.at[stage, d],
                device,
            )
            for d, device in enumerate(devices)
        ]
        sum_in[stage, me] = value
        if stage == 1:
            values, _ = end_corners(1, coarse, corner_copies, sums)
            field = corrected(local, values)
            copies = start_sides(3, field)
        for copy in group:
            copy.wait_recv()
        value = sum_in[stage, 0]
        for k in range(1, count):
            value = value + sum_in[stage, k]

    used = lax.broadcasted_iota(jnp.int32, value.shape, 1) < loads
    value = jnp.where(used, value, 1.0)
    rz, zq, ru, qu, zv, uv = (value[k : k + 1] for k in range(6))
    alpha = rz / zq
    new = alpha * (alpha * qu - ru)
    grown = 1.0 + new / rz
    energy = grown * grown * zq - alpha * grown * (zv + qu) + alpha * alpha * uv
    second = new / energy
    main = alpha + second * grown
    rest = second * alpha
    at = lax.broadcasted_iota(jnp.int32, (edge, edge), 0)
    factors = jnp.transpose(jnp.where(at == 0, main, rest))
    main, rest = factors[:loads, 0:1], factors[:loads, 1:2]
    mult_ref[...] = main * z_own - rest * u_own
    v_own = own(end_sides(3, field, copies))
    res_ref[...] = r_own - main * q_own + rest * v_own

    for copy in sends:
        copy.wait_send()


def body(
    dual_rhs,
    local_inverse,
    dirichlet,
    coarse_basis,
    coarse_inverse,
    corner_slot,
    side_map,
    edge_flip,
):
    loads, pair = dual_rhs.shape[2:]
    edge = pair // 2
    total = 4 * edge
    corner = coarse_inverse.shape[-1]
    n_wide, n_blk = lax.axis_size("wide"), lax.axis_size("blk")
    line = 8
    n_y = n_wide // line
    most = max(line, n_y, n_blk)
    small = (corner // 2, 2 * corner)
    dma = pltpu.SemaphoreType.DMA
    vmem = pl.BlockSpec(memory_space=pltpu.VMEM)
    anywhere = pl.BlockSpec(memory_space=pl.ANY)
    out = jax.ShapeDtypeStruct((loads, pair), F32)
    multipliers, residual = pl.pallas_call(
        functools.partial(kernel, line),
        out_shape=(out, out),
        in_specs=[anywhere] * 8,
        out_specs=(vmem, vmem),
        scratch_shapes=[
            pltpu.SMEM((1, n_wide), jnp.int32),
            pltpu.SMEM((1, 2), jnp.int32),
            pltpu.VMEM((1, total), jnp.int32),
            pltpu.VMEM((loads, pair), F32),
            pltpu.VMEM((corner, corner), F32),
            pltpu.VMEM((total, total), BF16),
            pltpu.VMEM((total, total), BF16),
            pltpu.VMEM((total, 4 * corner), BF16),
            dma((8,)),
            pltpu.VMEM((2, loads + 8, edge), F32),
            pltpu.VMEM((2, loads + 8, edge), F32),
            dma((2,)),
            dma((2,)),
            pltpu.VMEM((4, 4, loads, edge), F32),
            pltpu.VMEM((4, 4, loads, edge), F32),
            dma((4, 4)),
            dma((4, 4)),
            pltpu.VMEM((4, edge, 4 * corner), BF16),
            pltpu.VMEM((4, edge, 4 * corner), BF16),
            dma((4,)),
            dma((4,)),
            pltpu.VMEM((2, len(PARTNERS), 4, loads // 2, 2 * corner), BF16),
            pltpu.VMEM((2, len(PARTNERS), 4, loads // 2, 2 * corner), BF16),
            dma((2, 2, len(PARTNERS))),
            dma((2, 2, len(PARTNERS))),
            pltpu.VMEM((line,) + small, BF16),
            pltpu.VMEM((n_y, 2) + small, BF16),
            pltpu.VMEM((n_y, 2) + small, BF16),
            pltpu.VMEM((3,) + small, BF16),
            pltpu.VMEM((2,) + small, BF16),
            dma((3, most)),
            dma((3, most)),
            pltpu.VMEM((3, 8, edge), F32),
            pltpu.VMEM((3, most, 8, edge), F32),
            dma((3, most)),
            dma((3, most)),
        ],
        compiler_params=pltpu.CompilerParams(collective_id=0, has_side_effects=True),
        name="krylov",
    )(
        corner_slot,
        edge_flip[0],
        side_map[0],
        dual_rhs[0, 0],
        coarse_inverse[0, 0],
        dirichlet[0, 0],
        local_inverse[0, 0],
        coarse_basis[0, 0],
    )
    return (multipliers[None, None], residual[None, None])


def solution(mesh):
    in_specs = (
        P("wide", "blk", None, None),
        P("wide", "blk", None, None),
        P("wide", "blk", None, None),
        P("wide", "blk", None, None),
        P("wide", "blk", None, None),
        P("blk", None),
        P("wide", "blk", None),
        P("wide", "blk", None),
    )
    out_specs = (P("wide", "blk", None, None), P("wide", "blk", None, None))
    return jax.shard_map(body, mesh=mesh, in_specs=in_specs, out_specs=out_specs, check_vma=False)
```

```python
import functools

import jax
import jax.numpy as jnp
from jax import lax
from jax.experimental import pallas as pl
from jax.experimental.pallas import tpu as pltpu
from jax.sharding import PartitionSpec as P

MESH = pl.DeviceIdType.MESH
F32 = jnp.float32
BF16 = jnp.bfloat16
LEFT, RIGHT, LOWER, UPPER = range(4)
LL, LR, UL, UR = range(4)
CORNERS = [(-1, 0), (0, 0), (-1, 1), (0, 1)]
CROSS = [(0, 0), (-1, 0), (1, 0), (0, -1), (0, 1)]


def moved(step, by):
    return (step[0] + by[0], step[1] + by[1])


REACHED = sorted({moved(patch, corner) for patch in CROSS for corner in CORNERS})
PARTNERS = []
for _a in range(-2, 3):
    for _b in range(-2, 3):
        _shared = [k for k in range(4) if moved((_a, _b), CORNERS[k]) in REACHED]
        if (_a, _b) != (0, 0) and _shared:
            PARTNERS.append(((_a, _b), sorted(_shared, key=lambda k: k != LR)))
PARTNERS.sort(key=lambda entry: -abs(entry[0][0]) - abs(entry[0][1]))


def halves(x):
    hi = x.astype(BF16)
    lo = (x - hi.astype(F32)).astype(BF16)
    return jnp.concatenate([hi, lo], axis=0)


def wide_dot(x, matrix, dims=(((1,), (0,)), ((), ()))):
    rows = x.shape[0]
    both = lax.dot_general(halves(x), matrix, dims, preferred_element_type=F32)
    return both[:rows] + both[rows:]


def packed(block):
    rows = block.shape[0] // 2
    return jnp.concatenate([block[:rows], block[rows:]], axis=1)


def unpacked(block):
    width = block.shape[1] // 2
    return jnp.concatenate([block[:, :width], block[:, width:]], axis=0)


def kernel(
    line,
    slot_hbm,
    flip_hbm,
    map_hbm,
    rhs_hbm,
    cinv_hbm,
    stiff_hbm,
    greens_hbm,
    basis_hbm,
    mult_ref,
    res_ref,
    slot_ref,
    flip_ref,
    map_ref,
    rhs_ref,
    cinv_ref,
    stiff_ref,
    greens_ref,
    basis_ref,
    load_sem,
    first_out,
    first_in,
    first_send,
    first_recv,
    side_out,
    side_in,
    side_send,
    side_recv,
    edge_out,
    edge_in,
    edge_send,
    edge_recv,
    corner_out,
    corner_in,
    corner_send,
    corner_recv,
    block_z,
    block_stage,
    block_y,
    block_own,
    block_up,
    block_send,
    block_recv,
    sum_out,
    sum_in,
    sum_send,
    sum_recv,
):
    loads = rhs_ref.shape[0]
    edge = rhs_ref.shape[1] // 2
    n_wide = lax.axis_size("wide")
    n_blk = lax.axis_size("blk")
    n_y = n_wide // line
    col = lax.axis_index("wide")
    row = lax.axis_index("blk")
    y, z = col // line, col % line
    right, left = (col + 1) % n_wide, (col + n_wide - 1) % n_wide
    above, below = (row + 1) % n_blk, (row + n_blk - 1) % n_blk

    along_z = [y * line + (z + d) % line for d in range(1, line)]
    along_y = [((y + d) % n_y) * line + z for d in range(1, n_y)]
    along_blk = [(row + d) % n_blk for d in range(1, n_blk)]

    barrier = pltpu.get_barrier_semaphore()
    friends = [(c, row) for c in along_z + along_y + [left, right]]
    friends += [(col, r) for r in along_blk]
    partner_at = [
        ((col + n_wide + a) % n_wide, (row + n_blk + b) % n_blk) for (a, b), _ in PARTNERS
    ]
    friends += [device for ((a, b), _), device in zip(PARTNERS, partner_at) if a and (b or abs(a) > 1)]
    for friend in friends:
        pl.semaphore_signal(barrier, inc=1, device_id=friend, device_id_type=MESH)
    loading = [
        pltpu.make_async_copy(source, target, load_sem.at[k])
        for k, (source, target) in enumerate(
            [
                (stiff_hbm, stiff_ref),
                (greens_hbm, greens_ref),
                (basis_hbm, basis_ref),
                (rhs_hbm, rhs_ref),
                (cinv_hbm, cinv_ref),
                (map_hbm, map_ref),
                (flip_hbm, flip_ref),
                (slot_hbm, slot_ref),
            ]
        )
    ]
    for k in (3, 6, 4, 5, 2, 0, 7, 1):
        loading[k].start()

    loading[3].wait()
    loading[6].wait()
    loading[4].wait()
    pl.semaphore_wait(barrier, len(friends))

    sends = []

    def send(source, target, send_sem, recv_sem, device):
        copy = pltpu.make_async_remote_copy(
            src_ref=source,
            dst_ref=target,
            send_sem=send_sem,
            recv_sem=recv_sem,
            device_id=device,
            device_id_type=MESH,
        )
        copy.start()
        sends.append(copy)
        return copy

    has_left = jnp.where(col > 0, 1.0, 0.0).astype(F32)
    has_right = jnp.where(col < n_wide - 1, 1.0, 0.0).astype(F32)

    own_right = rhs_ref[:, :edge] * has_right
    own_up = rhs_ref[:, edge:]
    first_out[0, :loads] = own_right
    first_out[1, :loads] = own_up
    for k in range(2):
        flag = flip_ref[0, k].astype(F32)
        first_out[k, loads:] = jnp.full((8, edge), 1.0, F32) * flag
    first = [
        send(first_out.at[k], first_in.at[k], first_send.at[k], first_recv.at[k], device)
        for k, device in enumerate([(right, row), (col, above)])
    ]

    block_own[0] = packed(cinv_ref[...]).astype(BF16)
    fetch_z = [
        send(block_own.at[0], block_z.at[z], block_send.at[0, d], block_recv.at[0, d], (c, row))
        for d, c in enumerate(along_z)
    ]
    block_z[z] = block_own[0]

    loading[5].wait()
    total = 4 * edge
    index = jnp.broadcast_to(map_ref[...], (8, total)).astype(F32)
    lane = lax.broadcasted_iota(jnp.int32, (8, total), 1)
    sign = jnp.where((lane // edge) % 2 == 0, -1.0, 1.0).astype(F32)
    columns = jnp.transpose(jnp.concatenate([index, sign], axis=0))
    index_row = map_ref[...]
    index_col = (columns[:, :1] + 0.5).astype(jnp.int32)
    perm_t = jnp.where(
        lax.broadcasted_iota(jnp.int32, (total, total), 0) == index_row, sign[:1], 0.0
    ).astype(BF16)
    perm = jnp.where(
        lax.broadcasted_iota(jnp.int32, (total, total), 1) == index_col, columns[:, 8:9], 0.0
    ).astype(BF16)

    def reordered(matrix):
        half = jnp.dot(perm, matrix, preferred_element_type=F32).astype(BF16)
        return jnp.dot(half, perm_t, preferred_element_type=F32).astype(BF16)

    loading[2].wait()
    basis = jnp.dot(perm, basis_ref[...], preferred_element_type=F32).astype(BF16)
    for k in range(4):
        edge_out[k] = basis[k * edge : (k + 1) * edge]
    plan = [
        (LEFT, RIGHT, (left, row)),
        (RIGHT, LEFT, (right, row)),
        (LOWER, UPPER, (col, below)),
        (UPPER, LOWER, (col, above)),
    ]
    fetch_edges = [
        send(edge_out.at[k], edge_in.at[there], edge_send.at[k], edge_recv.at[there], device)
        for k, there, device in plan
    ]
    loading[0].wait()
    stiff = reordered(0.25 * stiff_ref[...])

    for copy in first:
        copy.wait_recv()
    rows_at = lax.broadcasted_iota(jnp.int32, (edge, edge), 0)
    lanes_at = lax.broadcasted_iota(jnp.int32, (edge, edge), 1)
    keep = jnp.where(rows_at == lanes_at, 1.0, 0.0).astype(F32)
    back = jnp.where(rows_at + lanes_at == edge - 1, 1.0, 0.0).astype(F32)
    turns = [
        (keep + first_in[k, loads : loads + 1] * (back - keep)).astype(BF16) for k in range(2)
    ]

    def turned_rows(matrix):
        blocks = [matrix[k * edge : (k + 1) * edge] for k in range(4)]
        for k, turn in zip((LEFT, LOWER), turns):
            blocks[k] = jnp.dot(turn, blocks[k], preferred_element_type=F32).astype(BF16)
        return jnp.concatenate(blocks, axis=0)

    def turned_columns(matrix):
        blocks = [matrix[:, k * edge : (k + 1) * edge] for k in range(4)]
        for k, turn in zip((LEFT, LOWER), turns):
            blocks[k] = jnp.dot(blocks[k], turn, preferred_element_type=F32).astype(BF16)
        return jnp.concatenate(blocks, axis=1)

    stiff_ref[...] = turned_columns(turned_rows(stiff))

    block_at = lax.broadcasted_iota(jnp.int32, (1, total), 1) // edge
    mask = jnp.where(block_at == LEFT, has_left, jnp.where(block_at == RIGHT, has_right, 1.0))

    def start_sides(step, field):
        for k in range(4):
            side_out[step, k] = field[:, k * edge : (k + 1) * edge]
        return [
            send(
                side_out.at[step, k],
                side_in.at[step, there],
                side_send.at[step, k],
                side_recv.at[step, there],
                device,
            )
            for k, there, device in plan
        ]

    def end_sides(step, field, copies):
        for copy in copies:
            copy.wait_recv()
        arrived = jnp.concatenate([side_in[step, k] for k in range(4)], axis=1)
        return (field + arrived) * mask

    x_rhs = jnp.concatenate(
        [first_in[0, :loads] * has_left, own_right, first_in[1, :loads], own_up], axis=1
    )
    field = wide_dot(x_rhs, stiff_ref[...])
    copies = start_sides(0, field)

    for copy in fetch_z:
        copy.wait_recv()
    loading[7].wait()
    for k in range(n_y):
        target = k * line + z
        behind = (target + n_wide - 1) % n_wide
        block_stage[k, 0] = block_z[slot_ref[0, target] % line]
        block_stage[k, 1] = block_z[slot_ref[0, behind] % line]
    fetch_y = [
        send(
            block_stage.at[(y + d + 1) % n_y],
            block_y.at[y],
            block_send.at[1, d],
            block_recv.at[1, d],
            (c, row),
        )
        for d, c in enumerate(along_y)
    ]
    block_y[y] = block_stage[y]

    basis_ref[...] = turned_rows(basis)
    for copy in fetch_edges:
        copy.wait_recv()
    across = [edge_in[k] for k in range(4)]
    for k, side in enumerate((RIGHT, UPPER)):
        own_turn = (keep + flip_ref[0, k].astype(F32) * (back - keep)).astype(BF16)
        across[side] = jnp.dot(own_turn, across[side], preferred_element_type=F32).astype(BF16)
    beyond = jnp.where(col > 1, 1.0, 0.0).astype(F32)

    def start_corners(step, field, sides=None):
        copies = [], []
        whole, field = field, field * mask
        shares = [wide_dot(field, basis_ref[...])] + [
            wide_dot(field[:, k * edge : (k + 1) * edge], across[k]) for k in range(4)
        ]
        reached = {}
        for patch, share in zip(CROSS, shares):
            width = share.shape[1] // 4
            for k in range(4):
                place = moved(patch, CORNERS[k])
                block = packed(share[:, k * width : (k + 1) * width])
                reached[place] = reached[place] + block if place in reached else block
        for place in REACHED:
            if place[0] < 0:
                reached[place] = reached[place] * (has_left if place[0] == -1 else beyond)
        for m, (steps, shared) in enumerate(PARTNERS):
            for n, k in enumerate(shared):
                corner_out[step, m, n] = reached[moved(steps, CORNERS[k])].astype(BF16)
        for part in range(2):
            if part == 1 and sides is not None:
                sides += start_sides(2, whole)
            for m, ((_, shared), device) in enumerate(zip(PARTNERS, partner_at)):
                ahead = 1 if sides is not None and shared[0] == LR else 0
                first, last = (0, ahead) if part == 0 else (ahead, len(shared))
                if first < last:
                    rows = pl.ds(first, last - first)
                    copies[part].append(
                        send(
                            corner_out.at[step, m, rows],
                            corner_in.at[step, m, rows],
                            corner_send.at[step, part, m],
                            corner_recv.at[step, part, m],
                            device,
                        )
                    )
        return copies, [reached[place] for place in CORNERS]

    def own_corner(step, copies, sums):
        for copy in copies[0]:
            copy.wait_recv()
        total = sums[LR]
        for m, (_, shared) in enumerate(PARTNERS):
            if shared[0] == LR:
                total = total + corner_in[step, m, 0].astype(F32)
        return unpacked(total)

    def end_corners(step, coarse, copies, sums):
        for copy in copies[1]:
            copy.wait_recv()
        sums = list(sums)
        for m, (_, shared) in enumerate(PARTNERS):
            for n, k in enumerate(shared):
                sums[k] = sums[k] + corner_in[step, m, n].astype(F32)
        sums = [unpacked(block) for block in sums]
        values = wide_dot(jnp.concatenate(sums, axis=1), coarse)
        at = lax.broadcasted_iota(jnp.int32, (1, values.shape[1]), 1) // (values.shape[1] // 4)
        return values * jnp.where(at % 2 == 0, has_left, 1.0), sums[LR]

    def corrected(local, values):
        return local + wide_dot(values, basis_ref[...], (((1,), (1,)), ((), ())))

    corner_copies, sums = start_corners(0, field)
    loading[1].wait()
    greens_ref[...] = turned_columns(turned_rows(reordered(greens_ref[...])))
    for copy in fetch_y:
        copy.wait_recv()
    block_own[1] = block_y[slot_ref[0, left] // line, 1]
    block_own[2] = block_y[slot_ref[0, col] // line, 0]
    hand_down = send(
        block_own.at[pl.ds(1, 2)], block_up, block_send.at[2, 0], block_recv.at[2, 0], (col, below)
    )
    x_z = end_sides(0, field, copies)
    local = wide_dot(x_z, greens_ref[...])
    hand_down.wait_recv()
    quarter = [
        unpacked(block.astype(F32)) for block in (block_own[1], block_own[2], block_up[0], block_up[1])
    ]
    width = quarter[0].shape[0]
    nothing = jnp.zeros((width, width), F32)
    coarse = jnp.concatenate(
        [
            jnp.concatenate([quarter[k] if k == m else nothing for m in range(4)], axis=1)
            for k in range(4)
        ],
        axis=0,
    ).astype(BF16)
    values, z_corner = end_corners(0, coarse, corner_copies, sums)
    field = corrected(local, values)
    copies = start_sides(1, field)
    x_q = end_sides(1, field, copies)

    field = wide_dot(x_q, stiff_ref[...])
    copies = []
    corner_copies, sums = start_corners(1, field, copies)
    x_u = end_sides(2, field, copies)

    local = wide_dot(x_u, greens_ref[...])

    def own(x):
        return jnp.concatenate([x[:, edge : 2 * edge], x[:, 3 * edge :]], axis=1)

    r_own, z_own, q_own, u_own = own(x_rhs), own(x_z), own(x_q), own(x_u)

    def inner(a, b):
        return jnp.sum(a * b, axis=1, keepdims=True)

    dots = [inner(r_own, z_own), inner(z_own, q_own), inner(r_own, u_own), inner(q_own, u_own)]
    local_dots = [inner(x_z, local), inner(x_u, local)]
    u_corner = own_corner(1, corner_copies, sums)
    own_value = wide_dot(u_corner, quarter[LR].astype(BF16))
    dots += [
        dot + inner(corner, own_value) for dot, corner in zip(local_dots, (z_corner, u_corner))
    ]

    at = lax.broadcasted_iota(jnp.int32, (loads, edge), 1)
    table = jnp.zeros((loads, edge), F32)
    for k, dot in enumerate(dots):
        table = jnp.where(at == k, dot, table)
    table = jnp.concatenate([table, jnp.zeros((edge - loads, edge), F32)], axis=0)
    value = jnp.transpose(table)[:8]

    stages = [
        (row, n_blk, [(col, r) for r in along_blk]),
        (z, line, [(c, row) for c in along_z]),
        (y, n_y, [(c, row) for c in along_y]),
    ]
    for stage, (me, count, devices) in enumerate(stages):
        sum_out[stage] = value
        group = [
            send(
                sum_out.at[stage],
                sum_in.at[stage, me],
                sum_send.at[stage, d],
                sum_recv.at[stage, d],
                device,
            )
            for d, device in enumerate(devices)
        ]
        sum_in[stage, me] = value
        if stage == 1:
            values, _ = end_corners(1, coarse, corner_copies, sums)
            field = corrected(local, values)
            copies = start_sides(3, field)
        for copy in group:
            copy.wait_recv()
        value = sum_in[stage, 0]
        for k in range(1, count):
            value = value + sum_in[stage, k]

    used = lax.broadcasted_iota(jnp.int32, value.shape, 1) < loads
    value = jnp.where(used, value, 1.0)
    rz, zq, ru, qu, zv, uv = (value[k : k + 1] for k in range(6))
    alpha = rz / zq
    new = alpha * (alpha * qu - ru)
    grown = 1.0 + new / rz
    energy = grown * grown * zq - alpha * grown * (zv + qu) + alpha * alpha * uv
    second = new / energy
    main = alpha + second * grown
    rest = second * alpha
    at = lax.broadcasted_iota(jnp.int32, (edge, edge), 0)
    factors = jnp.transpose(jnp.where(at == 0, main, rest))
    main, rest = factors[:loads, 0:1], factors[:loads, 1:2]
    mult_ref[...] = main * z_own - rest * u_own
    v_own = own(end_sides(3, field, copies))
    res_ref[...] = r_own - main * q_own + rest * v_own

    for copy in sends:
        copy.wait_send()


def body(
    dual_rhs,
    local_inverse,
    dirichlet,
    coarse_basis,
    coarse_inverse,
    corner_slot,
    side_map,
    edge_flip,
):
    loads, pair = dual_rhs.shape[2:]
    edge = pair // 2
    total = 4 * edge
    corner = coarse_inverse.shape[-1]
    n_wide, n_blk = lax.axis_size("wide"), lax.axis_size("blk")
    line = 8
    n_y = n_wide // line
    most = max(line, n_y, n_blk)
    small = (corner // 2, 2 * corner)
    dma = pltpu.SemaphoreType.DMA
    vmem = pl.BlockSpec(memory_space=pltpu.VMEM)
    anywhere = pl.BlockSpec(memory_space=pl.ANY)
    out = jax.ShapeDtypeStruct((loads, pair), F32)
    multipliers, residual = pl.pallas_call(
        functools.partial(kernel, line),
        out_shape=(out, out),
        in_specs=[anywhere] * 8,
        out_specs=(vmem, vmem),
        scratch_shapes=[
            pltpu.SMEM((1, n_wide), jnp.int32),
            pltpu.SMEM((1, 2), jnp.int32),
            pltpu.VMEM((1, total), jnp.int32),
            pltpu.VMEM((loads, pair), F32),
            pltpu.VMEM((corner, corner), F32),
            pltpu.VMEM((total, total), BF16),
            pltpu.VMEM((total, total), BF16),
            pltpu.VMEM((total, 4 * corner), BF16),
            dma((8,)),
            pltpu.VMEM((2, loads + 8, edge), F32),
            pltpu.VMEM((2, loads + 8, edge), F32),
            dma((2,)),
            dma((2,)),
            pltpu.VMEM((4, 4, loads, edge), F32),
            pltpu.VMEM((4, 4, loads, edge), F32),
            dma((4, 4)),
            dma((4, 4)),
            pltpu.VMEM((4, edge, 4 * corner), BF16),
            pltpu.VMEM((4, edge, 4 * corner), BF16),
            dma((4,)),
            dma((4,)),
            pltpu.VMEM((2, len(PARTNERS), 4, loads // 2, 2 * corner), BF16),
            pltpu.VMEM((2, len(PARTNERS), 4, loads // 2, 2 * corner), BF16),
            dma((2, 2, len(PARTNERS))),
            dma((2, 2, len(PARTNERS))),
            pltpu.VMEM((line,) + small, BF16),
            pltpu.VMEM((n_y, 2) + small, BF16),
            pltpu.VMEM((n_y, 2) + small, BF16),
            pltpu.VMEM((3,) + small, BF16),
            pltpu.VMEM((2,) + small, BF16),
            dma((3, most)),
            dma((3, most)),
            pltpu.VMEM((3, 8, edge), F32),
            pltpu.VMEM((3, most, 8, edge), F32),
            dma((3, most)),
            dma((3, most)),
        ],
        compiler_params=pltpu.CompilerParams(collective_id=0, has_side_effects=True),
        name="krylov",
    )(
        corner_slot,
        edge_flip[0],
        side_map[0],
        dual_rhs[0, 0],
        coarse_inverse[0, 0],
        dirichlet[0, 0],
        local_inverse[0, 0],
        coarse_basis[0, 0],
    )
    return (multipliers[None, None], residual[None, None])


def solution(mesh):
    in_specs = (
        P("wide", "blk", None, None),
        P("wide", "blk", None, None),
        P("wide", "blk", None, None),
        P("wide", "blk", None, None),
        P("wide", "blk", None, None),
        P("blk", None),
        P("wide", "blk", None),
        P("wide", "blk", None),
    )
    out_specs = (P("wide", "blk", None, None), P("wide", "blk", None, None))
    return jax.shard_map(body, mesh=mesh, in_specs=in_specs, out_specs=out_specs, check_vma=False)
```
